32 devices in a mesh: gx: 16 (over z, x, core), gz: 2 (over y).
Axes of the slice: x: 2, y: 2, z: 4, core: 2. Of those that a mesh axis runs over, the one named last changes fastest.
Arguments:
- overdensity_ratio: float32 [2, 1024, 32, 128], P('gz', 'gx'), may hold values from 0.07 to 15
- thermal_state: float32 [2, 1024, 32, 128], P('gz', 'gx'), may hold values from 0.3 to 3
- residual_drift: float32 [2, 1024, 32, 128], P('gz', 'gx'), may hold values from -0.45 to 0.45
- peculiar_displacement: int32 [2, 1024, 32, 128], P('gz', 'gx'), may hold values from -4 to 4
- doppler_spread: int32 [32], replicated, may hold values from 1 to 4, as said below
Outputs:
- flux: float32 [2, 1024, 32, 128], P('gz', 'gx')
- scale: float32 [32, 128], P('gx')
The draws below stay inside these ranges and needn't reach their ends.
Inputs may be any that keep to these rules, and one draw needn't show every extreme that they name: `doppler_spread`: some column has half width 4.
All inputs are finite; a program needn't handle non-finite values.
Results may differ from the reference program's by a relative error of at most 0.0003.
Values sent between devices are 32-bit elements; how exact they have to be, the bound alone decides.
A program may use at most 64 MiB of HBM per device.

```python
import math
import jax
import jax.numpy as jnp
from jax import lax

SHEET_VOXELS = 128
OMAX = 4
WMAX = 4
ITERS = 8
REACH = 8
PIECE_SPAN = 1024
PIECE_TALLY = 2
SIGHTLINE_TOTAL = 32


def draw_overdensity_ratio(key, part):
    shape = (PIECE_TALLY, PIECE_SPAN, SIGHTLINE_TOTAL, SHEET_VOXELS)
    noise_key = jax.random.fold_in(key, 11)
    segment = lax.broadcasted_iota(jnp.float32, shape, 0)
    within = lax.broadcasted_iota(jnp.float32, shape, 1)
    position = (segment * PIECE_SPAN + within) / (PIECE_TALLY * PIECE_SPAN)
    inner = within / PIECE_SPAN
    base = jnp.exp(jax.random.uniform(noise_key, shape, jnp.float32, -1.6, 1.6))
    trend = jnp.exp(1.2 * (position - 0.5) + 0.8 * (inner - 0.5))
    return base * trend


def draw_doppler_spread(key, part):
    width_key = jax.random.fold_in(key, 21)
    spot_key = jax.random.fold_in(key, 22)
    widths = jax.random.randint(width_key, (SIGHTLINE_TOTAL,), 1, WMAX + 1)
    spot = jax.random.randint(spot_key, (), 0, SIGHTLINE_TOTAL)
    return jnp.where(jnp.arange(SIGHTLINE_TOTAL) == spot, WMAX, widths).astype(jnp.int32)


def place_ends(result, stream_key, least, largest):
    shape = result.shape
    place = [jax.random.randint(jax.random.fold_in(stream_key, axis), (), 0, shape[axis]) for axis in range(len(shape))]
    result = result.at[tuple(place)].set(least)
    longest = shape.index(max(shape))
    place[longest] = (place[longest] + 1) % shape[longest]
    return result.at[tuple(place)].set(largest)


def block_scale(key, dims, cuts, least, high):
    factor_of = 1.0
    for dim, shards_of in cuts:
        heights = jax.random.uniform(jax.random.fold_in(jax.random.fold_in(key, 6), dim), (shards_of,), jnp.float32, least / len(cuts), high / len(cuts))
        factor_of = factor_of * jnp.repeat(jnp.exp(heights), dims[dim] // shards_of).reshape((-1,) + (1,) * (len(dims) - 1 - dim))
    return factor_of


def setup_inputs(seed: int = 0) -> dict:
    streams_of = jax.random.split(jax.random.key(seed), 6)
    return {
        "overdensity_ratio": draw_overdensity_ratio(jax.random.fold_in(streams_of[5], 71), 0),
        "thermal_state": jnp.clip(jnp.exp(math.log(3.0) - 2.3025851 * jax.random.uniform(streams_of[1], (PIECE_TALLY, PIECE_SPAN, SIGHTLINE_TOTAL, SHEET_VOXELS), jnp.float32) ** block_scale(streams_of[1], (PIECE_TALLY, PIECE_SPAN, SIGHTLINE_TOTAL, SHEET_VOXELS), ((0, 2), (1, 16)), -0.2, 0.2)), 0.3, 3.0),
        "residual_drift": jnp.clip(jax.random.uniform(streams_of[2], (PIECE_TALLY, PIECE_SPAN, SIGHTLINE_TOTAL, SHEET_VOXELS), jnp.float32, -0.45, 0.45) * block_scale(streams_of[2], (PIECE_TALLY, PIECE_SPAN, SIGHTLINE_TOTAL, SHEET_VOXELS), ((0, 2), (1, 16)), -0.4, 0.0), -0.45, 0.45),
        "peculiar_displacement": place_ends(jax.random.randint(streams_of[3], (PIECE_TALLY, PIECE_SPAN, SIGHTLINE_TOTAL, SHEET_VOXELS), -OMAX, OMAX + 1), jax.random.fold_in(streams_of[3], 1), -OMAX, OMAX).astype(jnp.int32),
        "doppler_spread": draw_doppler_spread(jax.random.fold_in(streams_of[5], 71), 0),
    }


def prepare_arrays(overdensity_ratio, thermal_state, residual_drift, peculiar_displacement):
    inverted_quantity = 1.0 / (1.2 * jnp.sqrt(thermal_state))
    profile_factor = 0.05 * overdensity_ratio * overdensity_ratio * jnp.exp(-0.7 * jnp.log(thermal_state)) * inverted_quantity / math.sqrt(math.pi)
    central_voxel = peculiar_displacement.astype(jnp.float32) + residual_drift
    return (profile_factor, central_voxel, inverted_quantity)

def column_depth(column):
    profile_factor, central_voxel, inverted_quantity, shifts, width = column
    total = jnp.zeros(profile_factor.shape, jnp.float32)
    for step in range(2 * REACH + 1):
        shift = step - REACH
        gap = jnp.float32(shift) - central_voxel
        keep = jnp.abs(shift - shifts) <= width
        term = jnp.where(keep, profile_factor * jnp.exp(-jnp.square(gap * inverted_quantity)), jnp.float32(0.0))
        total = total + jnp.roll(term, shift, axis=0)
    return total

def reference(overdensity_ratio, thermal_state, residual_drift, peculiar_displacement, doppler_spread):
    shape = overdensity_ratio.shape
    profile_factor, central_voxel, inverted_quantity = prepare_arrays(overdensity_ratio, thermal_state, residual_drift, peculiar_displacement)
    length = shape[0] * shape[1]

    def lines(field):
        return jnp.transpose(field.reshape(length, shape[2], shape[3]), (1, 0, 2))
    tau_lines = lax.map(column_depth, (lines(profile_factor), lines(central_voxel), lines(inverted_quantity), lines(peculiar_displacement), doppler_spread))
    tau = jnp.transpose(tau_lines, (1, 0, 2)).reshape(shape)
    cells = jnp.float32(length)
    level = jnp.zeros((shape[2], shape[3]), jnp.float32)
    for step in range(ITERS):
        factor = jnp.exp(level)
        damped = jnp.exp(-factor[None, None] * tau)
        first = lax.optimization_barrier(jnp.sum(damped, axis=(0, 1)))
        second = lax.optimization_barrier(jnp.sum(tau * damped, axis=(0, 1)))
        level = level - 0.4 * (first / cells - 0.35) / (-factor * second / cells)
    scale = jnp.exp(level)
    return (jnp.exp(-scale[None, None] * tau), scale)
```

```python
import functools
import math

import jax
import jax.numpy as jnp
from jax import lax
from jax.experimental import pallas as pl
from jax.experimental.pallas import tpu as pltpu
from jax.sharding import PartitionSpec as P

ITERS = 8
REACH = 8
BAND = 4
GROUPS = 8
LOG2E = math.log2(math.e)
PEAK = 0.05 / (1.2 * math.sqrt(math.pi))


def spread_terms(overdensity, thermal, drift, masks):
    log_t = jnp.log(thermal)
    q = (LOG2E / 1.44) * jnp.exp2(log_t * (-LOG2E))
    rq = drift * q
    middle = (PEAK * overdensity * overdensity) * jnp.exp2(log_t * (-1.2 * LOG2E) - drift * rq)
    rq2 = rq + rq
    h2 = jnp.exp2(-2.0 * q)
    steps = [h2 * m for m in masks]
    sides = []
    for ratio in (jnp.exp2(rq2 - q), jnp.exp2(-rq2 - q)):
        term = middle
        side = []
        for j in range(BAND):
            if j:
                ratio = ratio * steps[j - 1]
            term = term * ratio
            side.append(term)
        sides.append(side)
    return sides[1][::-1] + [middle] + sides[0]


def route(terms, displacement):
    zero = jnp.zeros_like(terms[0])
    u = displacement + BAND
    bit0 = (u & 1) != 0
    bit1 = (u & 2) != 0
    low = u < 4
    mid = u < 8

    def shift(values, by, bit):
        size = len(values)
        out = []
        for i in range(size + by):
            here = values[i] if i < size else zero
            there = values[i - by] if i >= by else zero
            out.append(jnp.where(bit, there, here))
        return out

    v = shift(shift(terms, 1, bit0), 2, bit1)
    slots = []
    for i in range(2 * REACH + 1):
        a = v[i] if i < 12 else zero
        b = v[i - 4] if 4 <= i < 16 else zero
        c = v[i - 8] if 8 <= i else zero
        if i < 4:
            slots.append(jnp.where(low, a, zero))
        elif i < 8:
            slots.append(jnp.where(low, a, jnp.where(mid, b, zero)))
        elif i < 12:
            slots.append(jnp.where(low, a, jnp.where(mid, b, c)))
        elif i < 16:
            slots.append(jnp.where(low, zero, jnp.where(mid, b, c)))
        else:
            slots.append(jnp.where(mid, zero, c))
    return slots


def total_rows(value):
    for by in (4, 2, 1):
        value = value + pltpu.roll(value, by, 0)
    return value


def kernel(
    nx, nz,
    spread_ref, od_ref, th_ref, dr_ref, dp_ref,
    tau_ref, scale_ref,
    width_ref, fields, moves, ext, lines, arrived, edge_out, edge_in, row, rows,
    in_sem, edge_ssem, edge_rsem, line_ssem, line_rsem, row_ssem, row_rsem, out_sem, width_sem,
):
    length, columns, lanes = od_ref.shape
    tiles = columns // 8
    count = nx * nz
    high = nx // tiles
    groups = line_rsem.shape[0]
    team = count // groups
    inner = length - 2 * REACH
    gx = lax.axis_index("gx")
    gz = lax.axis_index("gz")
    me = gz * nx + gx
    holders = columns // nx
    holds = gz < holders

    def device(index):
        return {"gx": lax.rem(index, nx), "gz": lax.div(index, nx)}

    def wrap(index, size):
        return jnp.where(index >= size, index - size, index)

    barrier = pltpu.get_barrier_semaphore()
    for b in range(nz):
        @pl.loop(0 if b else 1, nx)
        def _(a, b=b):
            pl.semaphore_signal(
                barrier, inc=1,
                device_id={"gx": wrap(gx + a, nx), "gz": wrap(gz + b, nz)},
                device_id_type=pl.DeviceIdType.MESH,
            )

    def input_copies(t):
        at = pl.ds(pl.multiple_of(t * 8, 8), 8)
        found = [
            pltpu.make_async_copy(ref.at[:, at, :], fields.at[k, t], in_sem.at[k, t])
            for k, ref in enumerate((od_ref, th_ref, dr_ref))
        ]
        return found + [pltpu.make_async_copy(dp_ref.at[:, at, :], moves.at[t], in_sem.at[3, t])]

    width_copy = pltpu.make_async_copy(spread_ref, width_ref, width_sem)
    width_copy.start()

    @pl.loop(0, tiles)
    def _(t):
        for copy in input_copies(t):
            copy.start()

    before = device(lax.rem(me + count - 1, count))
    after = device(lax.rem(me + 1, count))

    def brick_rows(z, t):
        return pl.ds(pl.multiple_of(z * columns + t * 8, 8), 8)

    def line_rows(place, t):
        return pl.ds(t * 8 * length + place, 8, stride=length)

    def tile_masks(t):
        sublane = lax.broadcasted_iota(jnp.int32, (8, lanes), 0)
        width = jnp.zeros((8, lanes), jnp.int32)
        for s in range(8):
            width = jnp.where(sublane == s, width_ref[t * 8 + s], width)
        return [jnp.where(width >= j, 1.0, 0.0).astype(jnp.float32) for j in (2, 3, 4)]

    empty = (jnp.zeros((8, lanes), jnp.float32),) * (2 * REACH)

    def deposit(t):
        masks = tile_masks(t)

        def group(g, window):
            done = []
            for k in range(8):
                z = g * 8 + k
                terms = spread_terms(fields[0, t, z], fields[1, t, z], fields[2, t, z], masks)
                slots = route(terms, moves[t, z])
                window = [w + s for w, s in zip(window, slots)] + slots[len(window):]
                done.append(window[0])
                window = window[1:]
            return done, tuple(window)

        def body(g, window):
            done, window = group(g, window)

            @pl.when(g == 0)
            def _():
                for k in range(8):
                    edge_out[1, t, k] = done[k]

            @pl.when(g == 1)
            def _():
                for k in range(8):
                    ext[brick_rows(k, t), :] = done[k]

            @pl.when(g >= 2)
            def _():
                for k in range(8):
                    ext[brick_rows(g * 8 - 8 + k, t), :] = done[k]
                    lines[line_rows(g * 8 - 16 + k, t), :] = done[k]

            return window

        window = lax.fori_loop(0, length // 8, body, empty)
        for k in range(REACH):
            ext[brick_rows(length - REACH + k, t), :] = window[k]
            edge_out[0, t, k] = window[REACH + k]

    def edge_copies(t):
        return [
            pltpu.make_async_remote_copy(
                src_ref=edge_out.at[k, t], dst_ref=edge_in.at[k, t],
                send_sem=edge_ssem.at[k, t], recv_sem=edge_rsem.at[k, t],
                device_id=target, device_id_type=pl.DeviceIdType.MESH,
            )
            for k, target in enumerate((after, before))
        ]

    def send_lines(t, start, size):
        @pl.loop(0, 8)
        def _(step):
            s = lax.rem(step + me, 8)
            column = t * 8 + s
            hz = lax.div(s, high)
            hx = lax.rem(s, high) * tiles + lax.rem(t + (tiles - lax.rem(hz * (tiles // 2), tiles)), tiles)

            @pl.when(hz * nx + hx != me)
            def _():
                pltpu.make_async_remote_copy(
                    src_ref=lines.at[pl.ds(pl.multiple_of(column * length + start, 8), size)],
                    dst_ref=arrived.at[pl.ds(pl.multiple_of(me * length + start, 8), size)],
                    send_sem=line_ssem, recv_sem=line_rsem.at[lax.div(me, team)],
                    device_id={"gx": hx, "gz": hz}, device_id_type=pl.DeviceIdType.MESH,
                ).start()

    width_copy.wait()

    @pl.loop(0, tiles)
    def _(t):
        for copy in input_copies(t):
            copy.wait()
        deposit(t)

        @pl.when(t == 0)
        def _():
            pl.semaphore_wait(barrier, count - 1)

        for copy in edge_copies(t):
            copy.start()
        send_lines(t, 0, inner)

    @pl.loop(0, tiles)
    def _(t):
        for copy in edge_copies(t):
            copy.wait_recv()
        for k in range(REACH):
            low = ext[brick_rows(k, t), :] + edge_in[0, t, k]
            ext[brick_rows(k, t), :] = low
            lines[line_rows(inner + k, t), :] = low
            top = ext[brick_rows(length - REACH + k, t), :] + edge_in[1, t, k]
            ext[brick_rows(length - REACH + k, t), :] = top
            lines[line_rows(inner + REACH + k, t), :] = top
        send_lines(t, inner, 2 * REACH)

    tau_copy = pltpu.make_async_copy(ext, tau_ref, out_sem)
    tau_copy.start()

    my_column = lax.rem(gx + lax.rem(gz * (tiles // 2), tiles), tiles) * 8 + lax.div(gx, tiles) + high * gz

    def row_copy(target):
        return pltpu.make_async_remote_copy(
            src_ref=row.at[0], dst_ref=rows.at[my_column],
            send_sem=row_ssem, recv_sem=row_rsem,
            device_id=target, device_id_type=pl.DeviceIdType.MESH,
        )

    def wait_bytes(ref, sem):
        pltpu.make_async_copy(ref, ref, sem).wait()

    def block(m, i, sums):
        first, second = list(sums[:4]), list(sums[4:])
        for k in range(length // 8):
            tau = arrived[pl.ds(pl.multiple_of(i * length + 8 * k, 8), 8), :]
            damped = jnp.exp2(m * tau)
            first[k % 4] += damped
            second[k % 4] += tau * damped
        return tuple(first + second)

    @pl.when(holds)
    def _():
        cells = float(count * length)
        zeros = (jnp.zeros((8, lanes), jnp.float32),) * 8

        def next_level(level, factor, sums):
            first = total_rows((sums[0] + sums[1]) + (sums[2] + sums[3]))
            second = total_rows((sums[4] + sums[5]) + (sums[6] + sums[7]))
            return level - 0.4 * (first / cells - 0.35) / (-factor * second / cells)

        unit = jnp.full((8, lanes), -LOG2E, jnp.float32)
        own = lax.div(me, team)

        for k in range(length // 8):
            arrived[pl.ds(pl.multiple_of(me * length + 8 * k, 8), 8), :] = lines[
                pl.ds(pl.multiple_of(my_column * length + 8 * k, 8), 8), :
            ]

        def visit(g, sums):
            return lax.fori_loop(0, team, lambda i, sums: block(unit, g * team + i, sums), sums, unroll=min(team, 4))

        wait_bytes(arrived.at[pl.ds(0, (team - 1) * length)], line_rsem.at[own])
        sums = visit(own, zeros)

        def arrive(step, sums):
            g = lax.rem(own + step, groups)
            wait_bytes(arrived.at[pl.ds(0, team * length)], line_rsem.at[g])
            return visit(g, sums)

        sums = lax.fori_loop(1, groups, arrive, sums)
        level = next_level(jnp.zeros((8, lanes), jnp.float32), jnp.ones((8, lanes), jnp.float32), sums)

        def newton(_, level):
            factor = jnp.exp(level)
            m = factor * (-LOG2E)
            sums = lax.fori_loop(0, count, lambda i, sums: block(m, i, sums), zeros, unroll=min(count, 16))
            return next_level(level, factor, sums)

        level = lax.fori_loop(1, ITERS, newton, level)
        row[0] = jnp.exp(level)[0:1]
        rows[my_column] = row[0]

        for b in range(nz):
            @pl.loop(0 if b else 1, nx)
            def _(a, b=b):
                row_copy({"gx": wrap(gx + a, nx), "gz": wrap(gz + b, nz)}).start()

        wait_bytes(rows.at[pl.ds(0, columns - 1)], row_rsem)
        wait_bytes(lines.at[pl.ds(0, (columns - 1) * length)], line_ssem)
        wait_bytes(arrived.at[pl.ds(0, count - 1)], row_ssem)

    @pl.when(jnp.logical_not(holds))
    def _():
        wait_bytes(rows, row_rsem)
        wait_bytes(lines, line_ssem)

    for x in range(columns):
        scale_ref[x:x + 1, :] = rows[x]

    @pl.loop(0, tiles)
    def _(t):
        for copy in edge_copies(t):
            copy.wait_send()

    tau_copy.wait()


def shards(nx, nz, overdensity_ratio, thermal_state, residual_drift, peculiar_displacement, doppler_spread):
    _, length, columns, lanes = overdensity_ratio.shape
    tiles = columns // 8
    count = nx * nz
    assert columns % 8 == 0 and nx % tiles == 0 and columns % nx == 0 and columns // nx <= nz
    assert length % 8 == 0 and length > 2 * REACH and count % GROUPS == 0 and count > GROUPS
    f32 = jnp.float32
    scratch = [
        pltpu.SMEM((columns,), jnp.int32),
        pltpu.VMEM((3, tiles, length, 8, lanes), f32),
        pltpu.VMEM((tiles, length, 8, lanes), jnp.int32),
        pltpu.VMEM((length * columns, lanes), f32),
        pltpu.VMEM((columns * length, lanes), f32),
        pltpu.VMEM((count * length, lanes), f32),
        pltpu.VMEM((2, tiles, REACH, 8, lanes), f32),
        pltpu.VMEM((2, tiles, REACH, 8, lanes), f32),
        pltpu.VMEM((1, 1, lanes), f32),
        pltpu.VMEM((columns, 1, lanes), f32),
        pltpu.SemaphoreType.DMA((4, tiles)),
        pltpu.SemaphoreType.DMA((2, tiles)),
        pltpu.SemaphoreType.DMA((2, tiles)),
        pltpu.SemaphoreType.DMA(()),
        pltpu.SemaphoreType.DMA((GROUPS,)),
    ] + [pltpu.SemaphoreType.DMA(())] * 4
    used = 4 * lanes * (columns * length * 6 + 2 * REACH * columns * 4 + count * length)
    bricks = [
        pltpu.with_memory_space_constraint(value[0], pltpu.HBM)
        for value in (overdensity_ratio, thermal_state, residual_drift, peculiar_displacement)
    ]
    tau, scale = pl.pallas_call(
        functools.partial(kernel, nx, nz),
        out_shape=(
            jax.ShapeDtypeStruct((length * columns, lanes), f32),
            jax.ShapeDtypeStruct((columns, lanes), f32),
        ),
        in_specs=[pl.BlockSpec(memory_space=pltpu.HBM)] * 5,
        out_specs=(pl.BlockSpec(memory_space=pl.ANY), pl.BlockSpec(memory_space=pltpu.VMEM)),
        scratch_shapes=scratch,
        compiler_params=pltpu.CompilerParams(
            collective_id=0, has_side_effects=True, vmem_limit_bytes=used + (4 << 20)
        ),
        name="forest",
    )(pltpu.with_memory_space_constraint(doppler_spread, pltpu.HBM), *bricks)
    flux = jnp.exp(-scale[None] * tau.reshape(length, columns, lanes))
    share = columns // nx
    return flux[None], lax.dynamic_slice_in_dim(scale, lax.axis_index("gx") * share, share, 0)


def solution(mesh):
    placed = (
        P("gz", "gx", None, None),
        P("gz", "gx", None, None),
        P("gz", "gx", None, None),
        P("gz", "gx", None, None),
        P(),
    )
    return jax.shard_map(
        functools.partial(shards, mesh.shape["gx"], mesh.shape["gz"]),
        mesh=mesh,
        in_specs=placed,
        out_specs=(P("gz", "gx", None, None), P("gx", None)),
        check_vma=False,
    )
```

```python
import functools
import math

import jax
import jax.numpy as jnp
from jax import lax
from jax.experimental import pallas as pl
from jax.experimental.pallas import tpu as pltpu
from jax.sharding import PartitionSpec as P

ITERS = 8
REACH = 8
BAND = 4
GROUPS = 8
PARTS = 4
LOG2E = math.log2(math.e)
PEAK = 0.05 / (1.2 * math.sqrt(math.pi))


def spread_terms(overdensity, thermal, drift, masks):
    log_t = jnp.log(thermal)
    q = (LOG2E / 1.44) * jnp.exp2(log_t * (-LOG2E))
    rq = drift * q
    middle = (PEAK * overdensity * overdensity) * jnp.exp2(log_t * (-1.2 * LOG2E) - drift * rq)
    rq2 = rq + rq
    h2 = jnp.exp2(-2.0 * q)
    steps = [h2 * m for m in masks]
    sides = []
    for ratio in (jnp.exp2(rq2 - q), jnp.exp2(-rq2 - q)):
        term = middle
        side = []
        for j in range(BAND):
            if j:
                ratio = ratio * steps[j - 1]
            term = term * ratio
            side.append(term)
        sides.append(side)
    return sides[1][::-1] + [middle] + sides[0]


def route(terms, displacement):
    zero = jnp.zeros_like(terms[0])
    u = displacement + BAND
    bit0 = (u & 1) != 0
    bit1 = (u & 2) != 0
    low = u < 4
    mid = u < 8

    def shift(values, by, bit):
        size = len(values)
        out = []
        for i in range(size + by):
            here = values[i] if i < size else zero
            there = values[i - by] if i >= by else zero
            out.append(jnp.where(bit, there, here))
        return out

    v = shift(shift(terms, 1, bit0), 2, bit1)
    slots = []
    for i in range(2 * REACH + 1):
        a = v[i] if i < 12 else zero
        b = v[i - 4] if 4 <= i < 16 else zero
        c = v[i - 8] if 8 <= i else zero
        if i < 4:
            slots.append(jnp.where(low, a, zero))
        elif i < 8:
            slots.append(jnp.where(low, a, jnp.where(mid, b, zero)))
        elif i < 12:
            slots.append(jnp.where(low, a, jnp.where(mid, b, c)))
        elif i < 16:
            slots.append(jnp.where(low, zero, jnp.where(mid, b, c)))
        else:
            slots.append(jnp.where(mid, zero, c))
    return slots


def total_rows(value):
    for by in (4, 2, 1):
        value = value + pltpu.roll(value, by, 0)
    return value


def kernel(
    nx, nz,
    spread_ref, od_ref, th_ref, dr_ref, dp_ref,
    tau_ref, scale_ref,
    width_ref, fields, moves, ext, lines, arrived, edge_out, edge_in, row, rows,
    in_sem, edge_ssem, edge_rsem, line_ssem, line_rsem, row_ssem, row_rsem, out_sem, width_sem, ready,
):
    length, columns, lanes = od_ref.shape
    tiles = columns // 8
    count = nx * nz
    half = tiles // 2
    holders = columns // nx
    high = 8 // holders
    middle = nx // 4
    groups = line_rsem.shape[0]
    team = count // groups
    inner = length - 2 * REACH
    gx = lax.axis_index("gx")
    gz = lax.axis_index("gz")
    me = gz * nx + gx
    holds = gz < holders
    inner_me = jnp.logical_and(gx >= middle, gx < nx - middle)

    def device(index):
        return {"gx": lax.rem(index, nx), "gz": lax.div(index, nx)}

    def wrap(index, size):
        return jnp.where(index >= size, index - size, index)

    barrier = pltpu.get_barrier_semaphore()
    for b in range(nz):
        @pl.loop(0 if b else 1, nx)
        def _(a, b=b):
            x = wrap(gx + a, nx)

            @pl.when(jnp.logical_or(inner_me, jnp.logical_or(x < middle, x >= nx - middle)))
            def _():
                pl.semaphore_signal(
                    barrier, inc=1, device_id={"gx": x, "gz": wrap(gz + b, nz)},
                    device_id_type=pl.DeviceIdType.MESH,
                )

    def meet():
        @pl.when(inner_me)
        def _():
            pl.semaphore_wait(barrier, count // 2 - 1)

        @pl.when(jnp.logical_not(inner_me))
        def _():
            pl.semaphore_wait(barrier, count - 1)
            for b in range(nz):
                @pl.loop(0, nx // 2)
                def _(a, b=b):
                    pl.semaphore_signal(
                        ready, inc=1, device_id={"gx": middle + a, "gz": wrap(gz + b, nz)},
                        device_id_type=pl.DeviceIdType.MESH,
                    )

    def meet_rest():
        @pl.when(inner_me)
        def _():
            pl.semaphore_wait(ready, count // 2)

    def tile_of(p):
        return jnp.where(p == 0, 0, jnp.where(p <= half, half + p - 1, p - half))

    def input_copies(t):
        at = pl.ds(pl.multiple_of(t * 8, 8), 8)
        found = [
            pltpu.make_async_copy(ref.at[:, at, :], fields.at[k, t], in_sem.at[k, t])
            for k, ref in enumerate((od_ref, th_ref, dr_ref))
        ]
        return found + [pltpu.make_async_copy(dp_ref.at[:, at, :], moves.at[t], in_sem.at[3, t])]

    width_copy = pltpu.make_async_copy(spread_ref, width_ref, width_sem)
    width_copy.start()

    @pl.loop(0, tiles)
    def _(p):
        for copy in input_copies(tile_of(p)):
            copy.start()

    before = device(lax.rem(me + count - 1, count))
    after = device(lax.rem(me + 1, count))

    def brick_rows(z, t):
        return pl.ds(pl.multiple_of(z * columns + t * 8, 8), 8)

    def line_rows(place, t):
        return pl.ds(t * 8 * length + place, 8, stride=length)

    def tile_masks(t):
        sublane = lax.broadcasted_iota(jnp.int32, (8, lanes), 0)
        width = jnp.zeros((8, lanes), jnp.int32)
        for s in range(8):
            width = jnp.where(sublane == s, width_ref[t * 8 + s], width)
        return [jnp.where(width >= j, 1.0, 0.0).astype(jnp.float32) for j in (2, 3, 4)]

    empty = (jnp.zeros((8, lanes), jnp.float32),) * (2 * REACH)

    def group(t, masks, g, window):
        done = []
        for k in range(8):
            z = g * 8 + k
            terms = spread_terms(fields[0, t, z], fields[1, t, z], fields[2, t, z], masks)
            slots = route(terms, moves[t, z])
            window = [w + s for w, s in zip(window, slots)] + slots[len(window):]
            done.append(window[0])
            window = window[1:]
        return done, tuple(window)

    def deposit(t, natural):
        masks = tile_masks(t)

        def body(g, window):
            done, window = group(t, masks, g, window)

            @pl.when(jnp.logical_and(g == 0, natural))
            def _():
                for k in range(8):
                    edge_out[1, t, k] = done[k]

            @pl.when(g == 1)
            def _():
                for k in range(8):
                    ext[brick_rows(k, t), :] = done[k]

            @pl.when(g >= 2)
            def _():
                for k in range(8):
                    ext[brick_rows(g * 8 - 8 + k, t), :] = done[k]
                    lines[line_rows(g * 8 - 16 + k, t), :] = done[k]

            return window

        window = lax.fori_loop(0, length // 8, body, empty)
        for k in range(REACH):
            ext[brick_rows(length - REACH + k, t), :] = window[k]

        @pl.when(natural)
        def _():
            for k in range(REACH):
                edge_out[0, t, k] = window[REACH + k]

    def early_edges(t):
        masks = tile_masks(t)

        @pl.loop(0, 2)
        def _(side):
            low = side == 1
            done, window = group(t, masks, jnp.where(low, 0, length // 8 - 1), empty)
            for k in range(REACH):
                edge_out[side, t, k] = jnp.where(low, done[k], window[REACH + k])

    def edge_copies(t):
        return [
            pltpu.make_async_remote_copy(
                src_ref=edge_out.at[k, t], dst_ref=edge_in.at[k, t],
                send_sem=edge_ssem.at[k, t], recv_sem=edge_rsem.at[k, t],
                device_id=target, device_id_type=pl.DeviceIdType.MESH,
            )
            for k, target in enumerate((after, before))
        ]

    def send_lines(t, start, size):
        @pl.loop(0, 8)
        def _(step):
            s = lax.rem(step + me, 8)
            column = t * 8 + s
            hz = lax.div(s, high)
            place = lax.rem(s, high) * half + lax.rem(t + hz, half)
            hx = jnp.where(t < half, middle + place, jnp.where(place < middle, place, place + 2 * middle))

            @pl.when(hz * nx + hx != me)
            def _():
                pltpu.make_async_remote_copy(
                    src_ref=lines.at[pl.ds(pl.multiple_of(column * length + start, 8), size)],
                    dst_ref=arrived.at[pl.ds(pl.multiple_of(me * length + start, 8), size)],
                    send_sem=line_ssem, recv_sem=line_rsem.at[lax.div(me, team)],
                    device_id={"gx": hx, "gz": hz}, device_id_type=pl.DeviceIdType.MESH,
                ).start()

    width_copy.wait()

    def add_edges(t):
        for copy in edge_copies(t):
            copy.wait_recv()
        for k in range(REACH):
            low = ext[brick_rows(k, t), :] + edge_in[0, t, k]
            ext[brick_rows(k, t), :] = low
            lines[line_rows(inner + k, t), :] = low
            top = ext[brick_rows(length - REACH + k, t), :] + edge_in[1, t, k]
            ext[brick_rows(length - REACH + k, t), :] = top
            lines[line_rows(inner + REACH + k, t), :] = top

    def wait_inputs(t):
        for copy in input_copies(t):
            copy.wait()

    def send_edges(t):
        for copy in edge_copies(t):
            copy.start()

    last = tile_of(tiles - 1)

    @pl.loop(0, tiles)
    def _(p):
        t = tile_of(p)

        @pl.when(p < tiles - 1)
        def _():
            wait_inputs(t)

        deposit(t, p < tiles - 1)

        @pl.when(p == 0)
        def _():
            meet()

        @pl.when(p == 1)
        def _():
            wait_inputs(last)
            early_edges(last)
            meet_rest()
            send_edges(tile_of(0))
            send_edges(last)

        @pl.when(jnp.logical_and(p > 0, p < tiles - 1))
        def _():
            send_edges(t)

        @pl.when(p < tiles - 1)
        def _():
            send_lines(t, 0, inner)

    @pl.loop(0, tiles)
    def _(p):
        t = tile_of(p)
        add_edges(t)

        @pl.when(p < tiles - 1)
        def _():
            send_lines(t, inner, 2 * REACH)

    send_lines(last, 0, length)

    tau_copy = pltpu.make_async_copy(ext, tau_ref, out_sem)
    tau_copy.start()

    place = jnp.where(inner_me, gx - middle, jnp.where(gx < middle, gx, gx - 2 * middle))
    my_tile = lax.rem(lax.rem(place, half) + half * nz - gz, half) + jnp.where(inner_me, 0, half)
    my_column = jnp.where(holds, my_tile * 8 + gz * high + lax.div(place, half), 0)

    def row_copy(target):
        return pltpu.make_async_remote_copy(
            src_ref=row.at[0], dst_ref=rows.at[my_column],
            send_sem=row_ssem, recv_sem=row_rsem,
            device_id=target, device_id_type=pl.DeviceIdType.MESH,
        )

    def wait_bytes(ref, sem):
        pltpu.make_async_copy(ref, ref, sem).wait()

    def block(m, i, sums):
        first, second = list(sums[:4]), list(sums[4:])
        for k in range(length // 8):
            tau = arrived[pl.ds(pl.multiple_of(i * length + 8 * k, 8), 8), :]
            damped = jnp.exp2(m * tau)
            first[k % 4] += damped
            second[k % 4] += tau * damped
        return tuple(first + second)

    @pl.when(holds)
    def _():
        cells = float(count * length)
        zeros = (jnp.zeros((8, lanes), jnp.float32),) * 8

        def next_level(level, factor, sums):
            first = total_rows((sums[0] + sums[1]) + (sums[2] + sums[3]))
            second = total_rows((sums[4] + sums[5]) + (sums[6] + sums[7]))
            return level - 0.4 * (first / cells - 0.35) / (-factor * second / cells)

        unit = jnp.full((8, lanes), -LOG2E, jnp.float32)
        own = lax.div(me, team)

        for k in range(length // 8):
            arrived[pl.ds(pl.multiple_of(me * length + 8 * k, 8), 8), :] = lines[
                pl.ds(pl.multiple_of(my_column * length + 8 * k, 8), 8), :
            ]

        def visit(g, sums):
            return lax.fori_loop(0, team, lambda i, sums: block(unit, g * team + i, sums), sums, unroll=min(team, 4))

        wait_bytes(arrived.at[pl.ds(0, (team - 1) * length)], line_rsem.at[own])
        sums = visit(own, zeros)

        def arrive(step, sums):
            g = lax.rem(own + step, groups)
            wait_bytes(arrived.at[pl.ds(0, team * length)], line_rsem.at[g])
            return visit(g, sums)

        sums = lax.fori_loop(1, groups, arrive, sums)
        level = next_level(jnp.zeros((8, lanes), jnp.float32), jnp.ones((8, lanes), jnp.float32), sums)

        def newton(_, level):
            factor = jnp.exp(level)
            m = factor * (-LOG2E)
            sums = lax.fori_loop(0, count, lambda i, sums: block(m, i, sums), zeros, unroll=min(count, 16))
            return next_level(level, factor, sums)

        level = lax.fori_loop(1, ITERS, newton, level)
        row[0] = jnp.exp(level)[0:1]
        rows[my_column] = row[0]

        for b in range(nz - 1, -1, -1):
            @pl.loop(0, nx)
            def _(a, b=b):
                x = jnp.where(gx < nx // 2, nx - 1 - a, a)

                @pl.when(jnp.logical_or(b > 0, x != gx))
                def _():
                    row_copy({"gx": x, "gz": wrap(gz + b, nz)}).start()

        wait_bytes(rows.at[pl.ds(0, columns - 1)], row_rsem)
        wait_bytes(lines.at[pl.ds(0, (columns - 1) * length)], line_ssem)
        wait_bytes(arrived.at[pl.ds(0, count - 1)], row_ssem)

    @pl.when(jnp.logical_not(holds))
    def _():
        wait_bytes(rows, row_rsem)
        wait_bytes(lines, line_ssem)

    for x in range(columns):
        scale_ref[x:x + 1, :] = rows[x]

    @pl.loop(0, tiles)
    def _(t):
        for copy in edge_copies(t):
            copy.wait_send()

    tau_copy.wait()


def transmit(share, tau_ref, scale_ref, flux_ref, part_ref, tau, scale, flux, in_sem, out_sem):
    columns, lanes = scale_ref.shape
    size = tau_ref.shape[0] // PARTS
    start = lax.axis_index("gx") * share
    parts = [pl.ds(i * size, size) for i in range(PARTS)]
    reads = [pltpu.make_async_copy(scale_ref, scale, in_sem.at[PARTS])]
    reads += [pltpu.make_async_copy(tau_ref.at[at], tau.at[at], in_sem.at[i]) for i, at in enumerate(parts)]
    writes = [pltpu.make_async_copy(scale_ref.at[pl.ds(start, share)], part_ref, out_sem.at[PARTS])]
    writes += [pltpu.make_async_copy(flux.at[at], flux_ref.at[at], out_sem.at[i]) for i, at in enumerate(parts)]
    for copy in reads:
        copy.start()
    writes[0].start()
    reads[0].wait()
    m = [scale[8 * t:8 * t + 8, :] * (-LOG2E) for t in range(columns // 8)]
    for i in range(PARTS):
        reads[i + 1].wait()

        @pl.loop(0, size // columns, unroll=True)
        def _(z, i=i):
            for t in range(columns // 8):
                at = pl.ds(pl.multiple_of(i * size + z * columns + 8 * t, 8), 8)
                flux[at, :] = jnp.exp2(m[t] * tau[at, :])

        writes[i + 1].start()
    for copy in writes:
        copy.wait()


def shards(nx, nz, overdensity_ratio, thermal_state, residual_drift, peculiar_displacement, doppler_spread):
    _, length, columns, lanes = overdensity_ratio.shape
    tiles = columns // 8
    count = nx * nz
    assert columns % 16 == 0 and nx % 4 == 0 and columns % nx == 0 and columns // nx <= nz
    assert 8 % (columns // nx) == 0
    assert length % 8 == 0 and length > 2 * REACH and count % GROUPS == 0 and count > GROUPS
    f32 = jnp.float32
    scratch = [
        pltpu.SMEM((columns,), jnp.int32),
        pltpu.VMEM((3, tiles, length, 8, lanes), f32),
        pltpu.VMEM((tiles, length, 8, lanes), jnp.int32),
        pltpu.VMEM((length * columns, lanes), f32),
        pltpu.VMEM((columns * length, lanes), f32),
        pltpu.VMEM((count * length, lanes), f32),
        pltpu.VMEM((2, tiles, REACH, 8, lanes), f32),
        pltpu.VMEM((2, tiles, REACH, 8, lanes), f32),
        pltpu.VMEM((1, 1, lanes), f32),
        pltpu.VMEM((columns, 1, lanes), f32),
        pltpu.SemaphoreType.DMA((4, tiles)),
        pltpu.SemaphoreType.DMA((2, tiles)),
        pltpu.SemaphoreType.DMA((2, tiles)),
        pltpu.SemaphoreType.DMA(()),
        pltpu.SemaphoreType.DMA((GROUPS,)),
    ] + [pltpu.SemaphoreType.DMA(())] * 4 + [pltpu.SemaphoreType.REGULAR]
    used = 4 * lanes * (columns * length * 6 + 2 * REACH * columns * 4 + count * length)
    bricks = [
        pltpu.with_memory_space_constraint(value[0], pltpu.HBM)
        for value in (overdensity_ratio, thermal_state, residual_drift, peculiar_displacement)
    ]
    tau, scale = pl.pallas_call(
        functools.partial(kernel, nx, nz),
        out_shape=(
            jax.ShapeDtypeStruct((length * columns, lanes), f32),
            jax.ShapeDtypeStruct((columns, lanes), f32),
        ),
        in_specs=[pl.BlockSpec(memory_space=pltpu.HBM)] * 5,
        out_specs=(pl.BlockSpec(memory_space=pl.ANY), pl.BlockSpec(memory_space=pltpu.VMEM)),
        scratch_shapes=scratch,
        compiler_params=pltpu.CompilerParams(
            collective_id=0, has_side_effects=True, vmem_limit_bytes=used + (4 << 20)
        ),
        name="forest",
    )(pltpu.with_memory_space_constraint(doppler_spread, pltpu.HBM), *bricks)
    share = columns // nx
    flux, part = pl.pallas_call(
        functools.partial(transmit, share),
        out_shape=(
            jax.ShapeDtypeStruct((length * columns, lanes), f32),
            jax.ShapeDtypeStruct((share, lanes), f32),
        ),
        in_specs=[pl.BlockSpec(memory_space=pl.ANY)] * 2,
        out_specs=(pl.BlockSpec(memory_space=pltpu.HBM), pl.BlockSpec(memory_space=pltpu.HBM)),
        scratch_shapes=[
            pltpu.VMEM((length * columns, lanes), f32), pltpu.VMEM((columns, lanes), f32),
            pltpu.VMEM((length * columns, lanes), f32),
            pltpu.SemaphoreType.DMA((PARTS + 1,)), pltpu.SemaphoreType.DMA((PARTS + 1,)),
        ],
        compiler_params=pltpu.CompilerParams(vmem_limit_bytes=8 * lanes * columns * (length + 1) + (4 << 20)),
        name="transmit",
    )(tau, scale)
    return flux.reshape(1, length, columns, lanes), part


def solution(mesh):
    placed = (
        P("gz", "gx", None, None),
        P("gz", "gx", None, None),
        P("gz", "gx", None, None),
        P("gz", "gx", None, None),
        P(),
    )
    return jax.shard_map(
        functools.partial(shards, mesh.shape["gx"], mesh.shape["gz"]),
        mesh=mesh,
        in_specs=placed,
        out_specs=(P("gz", "gx", None, None), P("gx", None)),
        check_vma=False,
    )
```

```python
import functools
import math

import jax
import jax.numpy as jnp
from jax import lax
from jax.experimental import pallas as pl
from jax.experimental.pallas import tpu as pltpu
from jax.sharding import PartitionSpec as P

ITERS = 8
REACH = 8
BAND = 4
GROUPS = 8
PARTS = 4
LOG2E = math.log2(math.e)
PEAK = 0.05 / (1.2 * math.sqrt(math.pi))


def spread_terms(overdensity, thermal, drift, masks):
    log_t = jnp.log(thermal)
    q = (LOG2E / 1.44) * jnp.exp2(log_t * (-LOG2E))
    rq = drift * q
    middle = (PEAK * overdensity * overdensity) * jnp.exp2(log_t * (-1.2 * LOG2E) - drift * rq)
    rq2 = rq + rq
    h2 = jnp.exp2(-2.0 * q)
    steps = [h2 * m for m in masks]
    sides = []
    for ratio in (jnp.exp2(rq2 - q), jnp.exp2(-rq2 - q)):
        term = middle
        side = []
        for j in range(BAND):
            if j:
                ratio = ratio * steps[j - 1]
            term = term * ratio
            side.append(term)
        sides.append(side)
    return sides[1][::-1] + [middle] + sides[0]


def route(terms, displacement):
    zero = jnp.zeros_like(terms[0])
    u = displacement + BAND
    bit0 = (u & 1) != 0
    bit1 = (u & 2) != 0
    low = u < 4
    mid = u < 8

    def shift(values, by, bit):
        size = len(values)
        out = []
        for i in range(size + by):
            here = values[i] if i < size else zero
            there = values[i - by] if i >= by else zero
            out.append(jnp.where(bit, there, here))
        return out

    v = shift(shift(terms, 1, bit0), 2, bit1)
    slots = []
    for i in range(2 * REACH + 1):
        a = v[i] if i < 12 else zero
        b = v[i - 4] if 4 <= i < 16 else zero
        c = v[i - 8] if 8 <= i else zero
        if i < 4:
            slots.append(jnp.where(low, a, zero))
        elif i < 8:
            slots.append(jnp.where(low, a, jnp.where(mid, b, zero)))
        elif i < 12:
            slots.append(jnp.where(low, a, jnp.where(mid, b, c)))
        elif i < 16:
            slots.append(jnp.where(low, zero, jnp.where(mid, b, c)))
        else:
            slots.append(jnp.where(mid, zero, c))
    return slots


def holder_order(nx, columns):
    half = columns // 16
    holders = columns // nx
    wide = 4 // holders
    used = [0] * 4
    order = []
    for low, high in [(1, 2)] + [(0, 3)] * half + [(1, 2)] * (half - 1):
        for hz in reversed(range(holders)):
            for block in (high, low):
                for w in reversed(range(wide)):
                    order.append((block * (nx // 4) + w * half + (used[block] + hz) % half, hz))
        used[low] += 1
        used[high] += 1
    return order


def total_rows(value):
    for by in (4, 2, 1):
        value = value + pltpu.roll(value, by, 0)
    return value


def kernel(
    nx, nz,
    spread_ref, od_ref, th_ref, dr_ref, dp_ref,
    tau_ref, scale_ref,
    width_ref, fields, moves, ext, lines, arrived, edge_out, edge_in, row, rows,
    in_sem, edge_ssem, edge_rsem, line_ssem, line_rsem, row_ssem, row_rsem, out_sem, width_sem, ready,
):
    length, columns, lanes = od_ref.shape
    tiles = columns // 8
    count = nx * nz
    holders = columns // nx
    middle = nx // 4
    order = holder_order(nx, columns)
    groups = line_rsem.shape[0]
    team = count // groups
    inner = length - 2 * REACH
    gx = lax.axis_index("gx")
    gz = lax.axis_index("gz")
    me = gz * nx + gx
    holds = gz < holders
    inner_me = jnp.logical_and(gx >= middle, gx < nx - middle)

    def device(index):
        return {"gx": lax.rem(index, nx), "gz": lax.div(index, nx)}

    def wrap(index, size):
        return jnp.where(index >= size, index - size, index)

    barrier = pltpu.get_barrier_semaphore()
    for b in range(nz):
        @pl.loop(0 if b else 1, nx)
        def _(a, b=b):
            x = wrap(gx + a, nx)

            @pl.when(jnp.logical_or(inner_me, jnp.logical_or(x < middle, x >= nx - middle)))
            def _():
                pl.semaphore_signal(
                    barrier, inc=1, device_id={"gx": x, "gz": wrap(gz + b, nz)},
                    device_id_type=pl.DeviceIdType.MESH,
                )

    def meet():
        @pl.when(inner_me)
        def _():
            pl.semaphore_wait(barrier, count // 2 - 1)

        @pl.when(jnp.logical_not(inner_me))
        def _():
            pl.semaphore_wait(barrier, count - 1)
            for b in range(nz):
                @pl.loop(0, nx // 2)
                def _(a, b=b):
                    pl.semaphore_signal(
                        ready, inc=1, device_id={"gx": middle + a, "gz": wrap(gz + b, nz)},
                        device_id_type=pl.DeviceIdType.MESH,
                    )

    def meet_rest():
        @pl.when(inner_me)
        def _():
            pl.semaphore_wait(ready, count // 2)

    def input_copies(t):
        at = pl.ds(pl.multiple_of(t * 8, 8), 8)
        found = [
            pltpu.make_async_copy(ref.at[:, at, :], fields.at[k, t], in_sem.at[k, t])
            for k, ref in enumerate((od_ref, th_ref, dr_ref))
        ]
        return found + [pltpu.make_async_copy(dp_ref.at[:, at, :], moves.at[t], in_sem.at[3, t])]

    width_copy = pltpu.make_async_copy(spread_ref, width_ref, width_sem)
    width_copy.start()

    @pl.loop(0, tiles)
    def _(p):
        for copy in input_copies(p):
            copy.start()

    before = device(lax.rem(me + count - 1, count))
    after = device(lax.rem(me + 1, count))

    def brick_rows(z, t):
        return pl.ds(pl.multiple_of(z * columns + t * 8, 8), 8)

    def line_rows(place, t):
        return pl.ds(t * 8 * length + place, 8, stride=length)

    def tile_masks(t):
        sublane = lax.broadcasted_iota(jnp.int32, (8, lanes), 0)
        width = jnp.zeros((8, lanes), jnp.int32)
        for s in range(8):
            width = jnp.where(sublane == s, width_ref[t * 8 + s], width)
        return [jnp.where(width >= j, 1.0, 0.0).astype(jnp.float32) for j in (2, 3, 4)]

    empty = (jnp.zeros((8, lanes), jnp.float32),) * (2 * REACH)

    def group(t, masks, g, window):
        done = []
        for k in range(8):
            z = g * 8 + k
            terms = spread_terms(fields[0, t, z], fields[1, t, z], fields[2, t, z], masks)
            slots = route(terms, moves[t, z])
            window = [w + s for w, s in zip(window, slots)] + slots[len(window):]
            done.append(window[0])
            window = window[1:]
        return done, tuple(window)

    def deposit(t, natural):
        masks = tile_masks(t)

        def body(g, window):
            done, window = group(t, masks, g, window)

            @pl.when(jnp.logical_and(g == 0, natural))
            def _():
                for k in range(8):
                    edge_out[1, t, k] = done[k]

            @pl.when(g == 1)
            def _():
                for k in range(8):
                    ext[brick_rows(k, t), :] = done[k]

            @pl.when(g >= 2)
            def _():
                for k in range(8):
                    ext[brick_rows(g * 8 - 8 + k, t), :] = done[k]
                    lines[line_rows(g * 8 - 16 + k, t), :] = done[k]

            return window

        window = lax.fori_loop(0, length // 8, body, empty)
        for k in range(REACH):
            ext[brick_rows(length - REACH + k, t), :] = window[k]

        @pl.when(natural)
        def _():
            for k in range(REACH):
                edge_out[0, t, k] = window[REACH + k]

    def early_edges(t):
        masks = tile_masks(t)

        @pl.loop(0, 2)
        def _(side):
            low = side == 1
            done, window = group(t, masks, jnp.where(low, 0, length // 8 - 1), empty)
            for k in range(REACH):
                edge_out[side, t, k] = jnp.where(low, done[k], window[REACH + k])

    def edge_copies(t):
        return [
            pltpu.make_async_remote_copy(
                src_ref=edge_out.at[k, t], dst_ref=edge_in.at[k, t],
                send_sem=edge_ssem.at[k, t], recv_sem=edge_rsem.at[k, t],
                device_id=target, device_id_type=pl.DeviceIdType.MESH,
            )
            for k, target in enumerate((after, before))
        ]

    def send_lines(t, start, size):
        for tile in range(tiles):
            @pl.when(t == tile)
            def _(tile=tile):
                for column in range(tile * 8, tile * 8 + 8):
                    hx, hz = order[column]

                    @pl.when(hz * nx + hx != me)
                    def _(column=column, hx=hx, hz=hz):
                        pltpu.make_async_remote_copy(
                            src_ref=lines.at[pl.ds(column * length + start, size)],
                            dst_ref=arrived.at[pl.ds(pl.multiple_of(me * length + start, 8), size)],
                            send_sem=line_ssem, recv_sem=line_rsem.at[lax.div(me, team)],
                            device_id={"gx": hx, "gz": hz}, device_id_type=pl.DeviceIdType.MESH,
                        ).start()

    width_copy.wait()

    def add_edges(t):
        for copy in edge_copies(t):
            copy.wait_recv()
        for k in range(REACH):
            low = ext[brick_rows(k, t), :] + edge_in[0, t, k]
            ext[brick_rows(k, t), :] = low
            lines[line_rows(inner + k, t), :] = low
            top = ext[brick_rows(length - REACH + k, t), :] + edge_in[1, t, k]
            ext[brick_rows(length - REACH + k, t), :] = top
            lines[line_rows(inner + REACH + k, t), :] = top

    def wait_inputs(t):
        for copy in input_copies(t):
            copy.wait()

    def send_edges(t):
        for copy in edge_copies(t):
            copy.start()

    last = tiles - 1

    @pl.loop(0, tiles)
    def _(p):
        t = p

        @pl.when(p < tiles - 1)
        def _():
            wait_inputs(t)

        deposit(t, p < tiles - 1)

        @pl.when(p == 0)
        def _():
            meet()

        @pl.when(p == 1)
        def _():
            wait_inputs(last)
            early_edges(last)
            meet_rest()
            send_edges(0)
            send_edges(last)

        @pl.when(jnp.logical_and(p > 0, p < tiles - 1))
        def _():
            send_edges(t)

        @pl.when(p < tiles - 1)
        def _():
            send_lines(t, 0, inner)

    @pl.loop(0, tiles)
    def _(p):
        t = p
        add_edges(t)

        @pl.when(p < tiles - 1)
        def _():
            send_lines(t, inner, 2 * REACH)

    send_lines(last, 0, length)

    tau_copy = pltpu.make_async_copy(ext, tau_ref, out_sem)
    tau_copy.start()

    my_column = 0
    for column, (hx, hz) in enumerate(order):
        my_column = jnp.where(me == hz * nx + hx, column, my_column)

    def row_copy(target):
        return pltpu.make_async_remote_copy(
            src_ref=row.at[0], dst_ref=rows.at[my_column],
            send_sem=row_ssem, recv_sem=row_rsem,
            device_id=target, device_id_type=pl.DeviceIdType.MESH,
        )

    def wait_bytes(ref, sem):
        pltpu.make_async_copy(ref, ref, sem).wait()

    def block(m, i, sums):
        first, second = list(sums[:4]), list(sums[4:])
        for k in range(length // 8):
            tau = arrived[pl.ds(pl.multiple_of(i * length + 8 * k, 8), 8), :]
            damped = jnp.exp2(m * tau)
            first[k % 4] += damped
            second[k % 4] += tau * damped
        return tuple(first + second)

    @pl.when(holds)
    def _():
        cells = float(count * length)
        zeros = (jnp.zeros((8, lanes), jnp.float32),) * 8

        def next_level(level, factor, sums):
            first = total_rows((sums[0] + sums[1]) + (sums[2] + sums[3]))
            second = total_rows((sums[4] + sums[5]) + (sums[6] + sums[7]))
            return level - 0.4 * (first / cells - 0.35) / (-factor * second / cells)

        unit = jnp.full((8, lanes), -LOG2E, jnp.float32)
        own = lax.div(me, team)

        for k in range(length // 8):
            arrived[pl.ds(pl.multiple_of(me * length + 8 * k, 8), 8), :] = lines[
                pl.ds(pl.multiple_of(my_column * length + 8 * k, 8), 8), :
            ]

        def visit(g, sums):
            return lax.fori_loop(0, team, lambda i, sums: block(unit, g * team + i, sums), sums, unroll=min(team, 4))

        wait_bytes(arrived.at[pl.ds(0, (team - 1) * length)], line_rsem.at[own])
        sums = visit(own, zeros)

        def arrive(step, sums):
            g = lax.rem(own + step, groups)
            wait_bytes(arrived.at[pl.ds(0, team * length)], line_rsem.at[g])
            return visit(g, sums)

        sums = lax.fori_loop(1, groups, arrive, sums)
        level = next_level(jnp.zeros((8, lanes), jnp.float32), jnp.ones((8, lanes), jnp.float32), sums)

        def newton(_, level):
            factor = jnp.exp(level)
            m = factor * (-LOG2E)
            sums = lax.fori_loop(0, count, lambda i, sums: block(m, i, sums), zeros, unroll=min(count, 16))
            return next_level(level, factor, sums)

        level = lax.fori_loop(1, ITERS, newton, level)
        row[0] = jnp.exp(level)[0:1]
        rows[my_column] = row[0]

        @pl.loop(0, nx)
        def _(x):
            for b in range(nz):
                @pl.when(jnp.logical_or(x != gx, gz != b))
                def _(b=b):
                    row_copy({"gx": x, "gz": b}).start()

        wait_bytes(rows.at[pl.ds(0, columns - 1)], row_rsem)
        wait_bytes(lines.at[pl.ds(0, (columns - 1) * length)], line_ssem)
        wait_bytes(arrived.at[pl.ds(0, count - 1)], row_ssem)

    @pl.when(jnp.logical_not(holds))
    def _():
        wait_bytes(rows, row_rsem)
        wait_bytes(lines, line_ssem)

    for x in range(columns):
        scale_ref[x:x + 1, :] = rows[x]

    @pl.loop(0, tiles)
    def _(t):
        for copy in edge_copies(t):
            copy.wait_send()

    tau_copy.wait()


def transmit(share, tau_ref, scale_ref, flux_ref, part_ref, tau, scale, flux, in_sem, out_sem):
    columns, lanes = scale_ref.shape
    size = tau_ref.shape[0] // PARTS
    start = lax.axis_index("gx") * share
    parts = [pl.ds(i * size, size) for i in range(PARTS)]
    reads = [pltpu.make_async_copy(scale_ref, scale, in_sem.at[PARTS])]
    reads += [pltpu.make_async_copy(tau_ref.at[at], tau.at[at], in_sem.at[i]) for i, at in enumerate(parts)]
    writes = [pltpu.make_async_copy(scale_ref.at[pl.ds(start, share)], part_ref, out_sem.at[PARTS])]
    writes += [pltpu.make_async_copy(flux.at[at], flux_ref.at[at], out_sem.at[i]) for i, at in enumerate(parts)]
    for copy in reads:
        copy.start()
    writes[0].start()
    reads[0].wait()
    m = [scale[8 * t:8 * t + 8, :] * (-LOG2E) for t in range(columns // 8)]
    for i in range(PARTS):
        reads[i + 1].wait()

        @pl.loop(0, size // columns, unroll=True)
        def _(z, i=i):
            for t in range(columns // 8):
                at = pl.ds(pl.multiple_of(i * size + z * columns + 8 * t, 8), 8)
                flux[at, :] = jnp.exp2(m[t] * tau[at, :])

        writes[i + 1].start()
    for copy in writes:
        copy.wait()


def shards(nx, nz, overdensity_ratio, thermal_state, residual_drift, peculiar_displacement, doppler_spread):
    _, length, columns, lanes = overdensity_ratio.shape
    tiles = columns // 8
    count = nx * nz
    assert columns % 16 == 0 and nx % 4 == 0 and columns % nx == 0 and columns // nx <= nz
    assert 8 % (columns // nx) == 0
    assert length % 8 == 0 and length > 2 * REACH and count % GROUPS == 0 and count > GROUPS
    f32 = jnp.float32
    scratch = [
        pltpu.SMEM((columns,), jnp.int32),
        pltpu.VMEM((3, tiles, length, 8, lanes), f32),
        pltpu.VMEM((tiles, length, 8, lanes), jnp.int32),
        pltpu.VMEM((length * columns, lanes), f32),
        pltpu.VMEM((columns * length, lanes), f32),
        pltpu.VMEM((count * length, lanes), f32),
        pltpu.VMEM((2, tiles, REACH, 8, lanes), f32),
        pltpu.VMEM((2, tiles, REACH, 8, lanes), f32),
        pltpu.VMEM((1, 1, lanes), f32),
        pltpu.VMEM((columns, 1, lanes), f32),
        pltpu.SemaphoreType.DMA((4, tiles)),
        pltpu.SemaphoreType.DMA((2, tiles)),
        pltpu.SemaphoreType.DMA((2, tiles)),
        pltpu.SemaphoreType.DMA(()),
        pltpu.SemaphoreType.DMA((GROUPS,)),
    ] + [pltpu.SemaphoreType.DMA(())] * 4 + [pltpu.SemaphoreType.REGULAR]
    used = 4 * lanes * (columns * length * 6 + 2 * REACH * columns * 4 + count * length)
    bricks = [
        pltpu.with_memory_space_constraint(value[0], pltpu.HBM)
        for value in (overdensity_ratio, thermal_state, residual_drift, peculiar_displacement)
    ]
    tau, scale = pl.pallas_call(
        functools.partial(kernel, nx, nz),
        out_shape=(
            jax.ShapeDtypeStruct((length * columns, lanes), f32),
            jax.ShapeDtypeStruct((columns, lanes), f32),
        ),
        in_specs=[pl.BlockSpec(memory_space=pltpu.HBM)] * 5,
        out_specs=(pl.BlockSpec(memory_space=pl.ANY), pl.BlockSpec(memory_space=pltpu.VMEM)),
        scratch_shapes=scratch,
        compiler_params=pltpu.CompilerParams(
            collective_id=0, has_side_effects=True, vmem_limit_bytes=used + (4 << 20)
        ),
        name="forest",
    )(pltpu.with_memory_space_constraint(doppler_spread, pltpu.HBM), *bricks)
    share = columns // nx
    flux, part = pl.pallas_call(
        functools.partial(transmit, share),
        out_shape=(
            jax.ShapeDtypeStruct((length * columns, lanes), f32),
            jax.ShapeDtypeStruct((share, lanes), f32),
        ),
        in_specs=[pl.BlockSpec(memory_space=pl.ANY)] * 2,
        out_specs=(pl.BlockSpec(memory_space=pltpu.HBM), pl.BlockSpec(memory_space=pltpu.HBM)),
        scratch_shapes=[
            pltpu.VMEM((length * columns, lanes), f32), pltpu.VMEM((columns, lanes), f32),
            pltpu.VMEM((length * columns, lanes), f32),
            pltpu.SemaphoreType.DMA((PARTS + 1,)), pltpu.SemaphoreType.DMA((PARTS + 1,)),
        ],
        compiler_params=pltpu.CompilerParams(vmem_limit_bytes=8 * lanes * columns * (length + 1) + (4 << 20)),
        name="transmit",
    )(tau, scale)
    return flux.reshape(1, length, columns, lanes), part


def solution(mesh):
    placed = (
        P("gz", "gx", None, None),
        P("gz", "gx", None, None),
        P("gz", "gx", None, None),
        P("gz", "gx", None, None),
        P(),
    )
    return jax.shard_map(
        functools.partial(shards, mesh.shape["gx"], mesh.shape["gz"]),
        mesh=mesh,
        in_specs=placed,
        out_specs=(P("gz", "gx", None, None), P("gx", None)),
        check_vma=False,
    )
```

```python
import functools
import math

import jax
import jax.numpy as jnp
from jax import lax
from jax.experimental import pallas as pl
from jax.experimental.pallas import tpu as pltpu
from jax.sharding import PartitionSpec as P

ITERS = 8
REACH = 8
BAND = 4
GROUPS = 8
PARTS = 4
LOG2E = math.log2(math.e)
PEAK = 0.05 / (1.2 * math.sqrt(math.pi))


def spread_terms(overdensity, thermal, drift, masks):
    log_t = jnp.log(thermal)
    q = (LOG2E / 1.44) * jnp.exp2(log_t * (-LOG2E))
    rq = drift * q
    middle = (PEAK * overdensity * overdensity) * jnp.exp2(log_t * (-1.2 * LOG2E) - drift * rq)
    rq2 = rq + rq
    h2 = jnp.exp2(-2.0 * q)
    steps = [h2 * m for m in masks]
    sides = []
    for ratio in (jnp.exp2(rq2 - q), jnp.exp2(-rq2 - q)):
        term = middle
        side = []
        for j in range(BAND):
            if j:
                ratio = ratio * steps[j - 1]
            term = term * ratio
            side.append(term)
        sides.append(side)
    return sides[1][::-1] + [middle] + sides[0]


def route(terms, displacement):
    zero = jnp.zeros_like(terms[0])
    u = displacement + BAND
    bit0 = (u & 1) != 0
    bit1 = (u & 2) != 0
    low = u < 4
    mid = u < 8

    def shift(values, by, bit):
        size = len(values)
        out = []
        for i in range(size + by):
            here = values[i] if i < size else zero
            there = values[i - by] if i >= by else zero
            out.append(jnp.where(bit, there, here))
        return out

    v = shift(shift(terms, 1, bit0), 2, bit1)
    slots = []
    for i in range(2 * REACH + 1):
        a = v[i] if i < 12 else zero
        b = v[i - 4] if 4 <= i < 16 else zero
        c = v[i - 8] if 8 <= i else zero
        if i < 4:
            slots.append(jnp.where(low, a, zero))
        elif i < 8:
            slots.append(jnp.where(low, a, jnp.where(mid, b, zero)))
        elif i < 12:
            slots.append(jnp.where(low, a, jnp.where(mid, b, c)))
        elif i < 16:
            slots.append(jnp.where(low, zero, jnp.where(mid, b, c)))
        else:
            slots.append(jnp.where(mid, zero, c))
    return slots


def holder_order(nx, columns):
    half = columns // 16
    holders = columns // nx
    wide = 4 // holders
    used = [0] * 4
    order = []
    for low, high in [(1, 2)] + [(0, 3)] * half + [(1, 2)] * (half - 1):
        for hz in reversed(range(holders)):
            for block in (high, low):
                for w in reversed(range(wide)):
                    order.append((block * (nx // 4) + w * half + (used[block] + hz) % half, hz))
        used[low] += 1
        used[high] += 1
    return order


def total_rows(value):
    for by in (4, 2, 1):
        value = value + pltpu.roll(value, by, 0)
    return value


def kernel(
    nx, nz,
    spread_ref, od_ref, th_ref, dr_ref, dp_ref,
    flux_ref, share_ref,
    width_ref, fields, moves, ext, lines, arrived, edge_out, edge_in, row, rows,
    in_sem, edge_ssem, edge_rsem, line_ssem, line_rsem, row_ssem, row_rsem, width_sem, ready,
):
    length, columns, lanes = od_ref.shape
    tiles = columns // 8
    count = nx * nz
    holders = columns // nx
    middle = nx // 4
    order = holder_order(nx, columns)
    groups = line_rsem.shape[0]
    team = count // groups
    inner = length - 2 * REACH
    gx = lax.axis_index("gx")
    gz = lax.axis_index("gz")
    me = gz * nx + gx
    holds = gz < holders
    inner_me = jnp.logical_and(gx >= middle, gx < nx - middle)

    def device(index):
        return {"gx": lax.rem(index, nx), "gz": lax.div(index, nx)}

    def wrap(index, size):
        return jnp.where(index >= size, index - size, index)

    barrier = pltpu.get_barrier_semaphore()
    for b in range(nz):
        @pl.loop(0 if b else 1, nx)
        def _(a, b=b):
            x = wrap(gx + a, nx)

            @pl.when(jnp.logical_or(inner_me, jnp.logical_or(x < middle, x >= nx - middle)))
            def _():
                pl.semaphore_signal(
                    barrier, inc=1, device_id={"gx": x, "gz": wrap(gz + b, nz)},
                    device_id_type=pl.DeviceIdType.MESH,
                )

    def meet():
        @pl.when(inner_me)
        def _():
            pl.semaphore_wait(barrier, count // 2 - 1)

        @pl.when(jnp.logical_not(inner_me))
        def _():
            pl.semaphore_wait(barrier, count - 1)
            for b in range(nz):
                @pl.loop(0, nx // 2)
                def _(a, b=b):
                    pl.semaphore_signal(
                        ready, inc=1, device_id={"gx": middle + a, "gz": wrap(gz + b, nz)},
                        device_id_type=pl.DeviceIdType.MESH,
                    )

    def meet_rest():
        @pl.when(inner_me)
        def _():
            pl.semaphore_wait(ready, count // 2)

    def input_copies(t):
        at = pl.ds(pl.multiple_of(t * 8, 8), 8)
        found = [
            pltpu.make_async_copy(ref.at[:, at, :], fields.at[k, t], in_sem.at[k, t])
            for k, ref in enumerate((od_ref, th_ref, dr_ref))
        ]
        return found + [pltpu.make_async_copy(dp_ref.at[:, at, :], moves.at[t], in_sem.at[3, t])]

    width_copy = pltpu.make_async_copy(spread_ref, width_ref, width_sem)
    width_copy.start()

    @pl.loop(0, tiles)
    def _(p):
        for copy in input_copies(p):
            copy.start()

    before = device(lax.rem(me + count - 1, count))
    after = device(lax.rem(me + 1, count))

    def brick_rows(z, t):
        return pl.ds(pl.multiple_of(z * columns + t * 8, 8), 8)

    def line_rows(place, t):
        return pl.ds(t * 8 * length + place, 8, stride=length)

    def tile_masks(t):
        sublane = lax.broadcasted_iota(jnp.int32, (8, lanes), 0)
        width = jnp.zeros((8, lanes), jnp.int32)
        for s in range(8):
            width = jnp.where(sublane == s, width_ref[t * 8 + s], width)
        return [jnp.where(width >= j, 1.0, 0.0).astype(jnp.float32) for j in (2, 3, 4)]

    empty = (jnp.zeros((8, lanes), jnp.float32),) * (2 * REACH)

    def group(t, masks, g, window):
        done = []
        for k in range(8):
            z = g * 8 + k
            terms = spread_terms(fields[0, t, z], fields[1, t, z], fields[2, t, z], masks)
            slots = route(terms, moves[t, z])
            window = [w + s for w, s in zip(window, slots)] + slots[len(window):]
            done.append(window[0])
            window = window[1:]
        return done, tuple(window)

    part = inner // 16 * 8

    def send_lines(t, start, size):
        for tile in range(tiles):
            @pl.when(t == tile)
            def _(tile=tile):
                for column in range(tile * 8, tile * 8 + 8):
                    hx, hz = order[column]

                    @pl.when(hz * nx + hx != me)
                    def _(column=column, hx=hx, hz=hz):
                        pltpu.make_async_remote_copy(
                            src_ref=lines.at[pl.ds(column * length + start, size)],
                            dst_ref=arrived.at[pl.ds(pl.multiple_of(me * length + start, 8), size)],
                            send_sem=line_ssem, recv_sem=line_rsem.at[lax.div(me, team)],
                            device_id={"gx": hx, "gz": hz}, device_id_type=pl.DeviceIdType.MESH,
                        ).start()

    def deposit(t, natural, first):
        masks = tile_masks(t)

        def body(g, window):
            done, window = group(t, masks, g, window)

            @pl.when(jnp.logical_and(g == 0, natural))
            def _():
                for k in range(8):
                    edge_out[1, t, k] = done[k]

            @pl.when(g == 1)
            def _():
                for k in range(8):
                    ext[brick_rows(k, t), :] = done[k]

            @pl.when(g >= 2)
            def _():
                for k in range(8):
                    ext[brick_rows(g * 8 - 8 + k, t), :] = done[k]
                    lines[line_rows(g * 8 - 16 + k, t), :] = done[k]

            @pl.when(jnp.logical_and(first, g == part // 8 + 1))
            def _():
                meet()
                send_lines(0, 0, part)

            return window

        window = lax.fori_loop(0, length // 8, body, empty)
        for k in range(REACH):
            ext[brick_rows(length - REACH + k, t), :] = window[k]

        @pl.when(natural)
        def _():
            for k in range(REACH):
                edge_out[0, t, k] = window[REACH + k]

    def early_edges(t):
        masks = tile_masks(t)

        @pl.loop(0, 2)
        def _(side):
            low = side == 1
            done, window = group(t, masks, jnp.where(low, 0, length // 8 - 1), empty)
            for k in range(REACH):
                edge_out[side, t, k] = jnp.where(low, done[k], window[REACH + k])

    def edge_copies(t):
        return [
            pltpu.make_async_remote_copy(
                src_ref=edge_out.at[k, t], dst_ref=edge_in.at[k, t],
                send_sem=edge_ssem.at[k, t], recv_sem=edge_rsem.at[k, t],
                device_id=target, device_id_type=pl.DeviceIdType.MESH,
            )
            for k, target in enumerate((after, before))
        ]

    width_copy.wait()

    def add_edges(t):
        for copy in edge_copies(t):
            copy.wait_recv()
        for k in range(REACH):
            low = ext[brick_rows(k, t), :] + edge_in[0, t, k]
            ext[brick_rows(k, t), :] = low
            lines[line_rows(inner + k, t), :] = low
            top = ext[brick_rows(length - REACH + k, t), :] + edge_in[1, t, k]
            ext[brick_rows(length - REACH + k, t), :] = top
            lines[line_rows(inner + REACH + k, t), :] = top

    def wait_inputs(t):
        for copy in input_copies(t):
            copy.wait()

    def send_edges(t):
        for copy in edge_copies(t):
            copy.start()

    last = tiles - 1

    @pl.loop(0, tiles)
    def _(p):
        t = p

        @pl.when(p < 2)
        def _():
            wait_inputs(t)

        deposit(t, p < 2, p == 0)

        @pl.when(p == 1)
        def _():
            @pl.loop(2, tiles)
            def _(q):
                wait_inputs(q)
                early_edges(q)

            meet_rest()

            @pl.loop(0, tiles)
            def _(q):
                send_edges(q)

        @pl.when(p == 0)
        def _():
            send_lines(0, part, inner - part)

        @pl.when(jnp.logical_and(p > 0, p < tiles - 1))
        def _():
            send_lines(t, 0, inner)

    @pl.loop(0, tiles)
    def _(p):
        t = p
        add_edges(t)

        @pl.when(p < tiles - 1)
        def _():
            send_lines(t, inner, 2 * REACH)

    send_lines(last, 0, length)

    my_column = 0
    for column, (hx, hz) in enumerate(order):
        my_column = jnp.where(me == hz * nx + hx, column, my_column)

    early = columns - 8
    my_class = jnp.where(my_column >= early, 1, 0)

    def row_copy(target):
        return pltpu.make_async_remote_copy(
            src_ref=row.at[0], dst_ref=rows.at[my_column],
            send_sem=row_ssem, recv_sem=row_rsem.at[my_class],
            device_id=target, device_id_type=pl.DeviceIdType.MESH,
        )

    def wait_bytes(ref, sem):
        pltpu.make_async_copy(ref, ref, sem).wait()

    def block(m, i, sums):
        first, second = list(sums[:4]), list(sums[4:])
        for k in range(length // 8):
            tau = arrived[pl.ds(pl.multiple_of(i * length + 8 * k, 8), 8), :]
            damped = jnp.exp2(m * tau)
            first[k % 4] += damped
            second[k % 4] += tau * damped
        return tuple(first + second)

    @pl.when(holds)
    def _():
        cells = float(count * length)
        zeros = (jnp.zeros((8, lanes), jnp.float32),) * 8

        def next_level(level, factor, sums):
            first = total_rows((sums[0] + sums[1]) + (sums[2] + sums[3]))
            second = total_rows((sums[4] + sums[5]) + (sums[6] + sums[7]))
            return level + (first * (0.4 / cells) - 0.14) / (factor * (second * (1.0 / cells)))

        unit = jnp.full((8, lanes), -LOG2E, jnp.float32)
        own = lax.div(me, team)

        for k in range(length // 8):
            arrived[pl.ds(pl.multiple_of(me * length + 8 * k, 8), 8), :] = lines[
                pl.ds(pl.multiple_of(my_column * length + 8 * k, 8), 8), :
            ]

        def visit(g, sums):
            return lax.fori_loop(0, team, lambda i, sums: block(unit, g * team + i, sums), sums, unroll=min(team, 4))

        wait_bytes(arrived.at[pl.ds(0, (team - 1) * length)], line_rsem.at[own])
        sums = visit(own, zeros)

        def arrive(step, sums):
            g = lax.rem(own + step, groups)
            wait_bytes(arrived.at[pl.ds(0, team * length)], line_rsem.at[g])
            return visit(g, sums)

        sums = lax.fori_loop(1, groups, arrive, sums)
        level = next_level(jnp.zeros((8, lanes), jnp.float32), jnp.ones((8, lanes), jnp.float32), sums)

        def newton(_, level):
            factor = jnp.exp(level)
            m = factor * (-LOG2E)
            sums = lax.fori_loop(0, count, lambda i, sums: block(m, i, sums), zeros, unroll=min(count, 16))
            return next_level(level, factor, sums)

        level = lax.fori_loop(1, ITERS, newton, level)
        row[0] = jnp.exp(level)[0:1]
        rows[my_column] = row[0]

        @pl.loop(0, nx)
        def _(x):
            for b in range(nz):
                @pl.when(jnp.logical_or(x != gx, gz != b))
                def _(b=b):
                    row_copy({"gx": x, "gz": b}).start()

    def wait_rows(kind, size):
        mine = jnp.logical_and(holds, my_class == kind)

        @pl.when(mine)
        def _():
            wait_bytes(rows.at[pl.ds(0, size - 1)], row_rsem.at[kind])

        @pl.when(jnp.logical_not(mine))
        def _():
            wait_bytes(rows.at[pl.ds(0, size)], row_rsem.at[kind])

    def transmit(t):
        m = jnp.concatenate([rows[t * 8 + x] for x in range(8)], axis=0) * (-LOG2E)

        @pl.loop(0, length // 16)
        def _(g):
            for k in range(16):
                at = brick_rows(g * 16 + k, t)
                flux_ref[at, :] = jnp.exp2(m * ext[at, :])

    wait_rows(0, early)

    @pl.loop(0, tiles - 1)
    def _(t):
        transmit(t)

    wait_rows(1, 8)
    transmit(tiles - 1)
    for x in range(share_ref.shape[0]):
        share_ref[x:x + 1, :] = rows[gx * share_ref.shape[0] + x]

    @pl.when(holds)
    def _():
        wait_bytes(lines.at[pl.ds(0, (columns - 1) * length)], line_ssem)
        wait_bytes(arrived.at[pl.ds(0, count - 1)], row_ssem)

    @pl.when(jnp.logical_not(holds))
    def _():
        wait_bytes(lines, line_ssem)

    @pl.loop(0, tiles)
    def _(t):
        for copy in edge_copies(t):
            copy.wait_send()


def deliver(flux_ref, part_ref, flux_out, part_out, sem):
    size = flux_ref.shape[0] // PARTS
    copies = [
        pltpu.make_async_copy(flux_ref.at[pl.ds(i * size, size)], flux_out.at[pl.ds(i * size, size)], sem.at[i])
        for i in range(PARTS)
    ]
    copies.append(pltpu.make_async_copy(part_ref, part_out, sem.at[PARTS]))
    for copy in copies:
        copy.start()
    for copy in copies:
        copy.wait()


def shards(nx, nz, overdensity_ratio, thermal_state, residual_drift, peculiar_displacement, doppler_spread):
    _, length, columns, lanes = overdensity_ratio.shape
    tiles = columns // 8
    count = nx * nz
    assert columns % 16 == 0 and nx % 4 == 0 and columns % nx == 0 and columns // nx <= nz
    assert 8 % (columns // nx) == 0
    assert length % 16 == 0 and length > 2 * REACH and count % GROUPS == 0 and count > GROUPS
    f32 = jnp.float32
    scratch = [
        pltpu.SMEM((columns,), jnp.int32),
        pltpu.VMEM((3, tiles, length, 8, lanes), f32),
        pltpu.VMEM((tiles, length, 8, lanes), jnp.int32),
        pltpu.VMEM((length * columns, lanes), f32),
        pltpu.VMEM((columns * length, lanes), f32),
        pltpu.VMEM((count * length, lanes), f32),
        pltpu.VMEM((2, tiles, REACH, 8, lanes), f32),
        pltpu.VMEM((2, tiles, REACH, 8, lanes), f32),
        pltpu.VMEM((1, 1, lanes), f32),
        pltpu.VMEM((columns, 1, lanes), f32),
        pltpu.SemaphoreType.DMA((4, tiles)),
        pltpu.SemaphoreType.DMA((2, tiles)),
        pltpu.SemaphoreType.DMA((2, tiles)),
        pltpu.SemaphoreType.DMA(()),
        pltpu.SemaphoreType.DMA((GROUPS,)),
        pltpu.SemaphoreType.DMA(()),
        pltpu.SemaphoreType.DMA((2,)),
        pltpu.SemaphoreType.DMA(()),
        pltpu.SemaphoreType.REGULAR,
    ]
    used = 4 * lanes * (columns * length * 6 + 2 * REACH * columns * 4 + count * length)
    bricks = [
        pltpu.with_memory_space_constraint(value[0], pltpu.HBM)
        for value in (overdensity_ratio, thermal_state, residual_drift, peculiar_displacement)
    ]
    flux, part = pl.pallas_call(
        functools.partial(kernel, nx, nz),
        out_shape=(
            jax.ShapeDtypeStruct((length * columns, lanes), f32),
            jax.ShapeDtypeStruct((columns // nx, lanes), f32),
        ),
        in_specs=[pl.BlockSpec(memory_space=pltpu.HBM)] * 5,
        out_specs=(pl.BlockSpec(memory_space=pltpu.VMEM), pl.BlockSpec(memory_space=pltpu.VMEM)),
        scratch_shapes=scratch,
        compiler_params=pltpu.CompilerParams(
            collective_id=0, has_side_effects=True, vmem_limit_bytes=used + 4 * lanes * columns * length + (4 << 20)
        ),
        name="forest",
    )(pltpu.with_memory_space_constraint(doppler_spread, pltpu.HBM), *bricks)
    flux, part = pl.pallas_call(
        deliver,
        out_shape=(
            jax.ShapeDtypeStruct((length * columns, lanes), f32),
            jax.ShapeDtypeStruct((columns // nx, lanes), f32),
        ),
        in_specs=[pl.BlockSpec(memory_space=pl.ANY)] * 2,
        out_specs=(pl.BlockSpec(memory_space=pltpu.HBM), pl.BlockSpec(memory_space=pltpu.HBM)),
        scratch_shapes=[pltpu.SemaphoreType.DMA((PARTS + 1,))],
        compiler_params=pltpu.CompilerParams(vmem_limit_bytes=1 << 20),
        name="deliver",
    )(flux, part)
    return flux.reshape(1, length, columns, lanes), part


def solution(mesh):
    placed = (
        P("gz", "gx", None, None),
        P("gz", "gx", None, None),
        P("gz", "gx", None, None),
        P("gz", "gx", None, None),
        P(),
    )
    return jax.shard_map(
        functools.partial(shards, mesh.shape["gx"], mesh.shape["gz"]),
        mesh=mesh,
        in_specs=placed,
        out_specs=(P("gz", "gx", None, None), P("gx", None)),
        check_vma=False,
    )
```

```python
import functools
import math

import jax
import jax.numpy as jnp
from jax import lax
from jax.experimental import pallas as pl
from jax.experimental.pallas import tpu as pltpu
from jax.sharding import PartitionSpec as P

ITERS = 8
REACH = 8
BAND = 4
GROUPS = 2
PARTS = 4
LOG2E = math.log2(math.e)
PEAK = 0.05 / (1.2 * math.sqrt(math.pi))


def spread_terms(overdensity, thermal, drift, masks):
    log_t = jnp.log(thermal)
    q = (LOG2E / 1.44) * jnp.exp2(log_t * (-LOG2E))
    rq = drift * q
    middle = (PEAK * overdensity * overdensity) * jnp.exp2(log_t * (-1.2 * LOG2E) - drift * rq)
    rq2 = rq + rq
    h2 = jnp.exp2(-2.0 * q)
    steps = [h2 * m for m in masks]
    sides = []
    for ratio in (jnp.exp2(rq2 - q), jnp.exp2(-rq2 - q)):
        term = middle
        side = []
        for j in range(BAND):
            if j:
                ratio = ratio * steps[j - 1]
            term = term * ratio
            side.append(term)
        sides.append(side)
    return sides[1][::-1] + [middle] + sides[0]


def route(terms, displacement):
    zero = jnp.zeros_like(terms[0])
    u = displacement + BAND
    bit0 = (u & 1) != 0
    bit1 = (u & 2) != 0
    low = u < 4
    mid = u < 8

    def shift(values, by, bit):
        size = len(values)
        out = []
        for i in range(size + by):
            here = values[i] if i < size else zero
            there = values[i - by] if i >= by else zero
            out.append(jnp.where(bit, there, here))
        return out

    v = shift(shift(terms, 1, bit0), 2, bit1)
    slots = []
    for i in range(2 * REACH + 1):
        a = v[i] if i < 12 else zero
        b = v[i - 4] if 4 <= i < 16 else zero
        c = v[i - 8] if 8 <= i else zero
        if i < 4:
            slots.append(jnp.where(low, a, zero))
        elif i < 8:
            slots.append(jnp.where(low, a, jnp.where(mid, b, zero)))
        elif i < 12:
            slots.append(jnp.where(low, a, jnp.where(mid, b, c)))
        elif i < 16:
            slots.append(jnp.where(low, zero, jnp.where(mid, b, c)))
        else:
            slots.append(jnp.where(mid, zero, c))
    return slots


def holder_order(nx, columns):
    half = columns // 16
    holders = columns // nx
    wide = 4 // holders
    used = [0] * 4
    order = []
    for low, high in [(1, 2)] + [(0, 3)] * half + [(1, 2)] * (half - 1):
        for hz in reversed(range(holders)):
            for block in (high, low):
                for w in reversed(range(wide)):
                    order.append((block * (nx // 4) + w * half + (used[block] + hz) % half, hz))
        used[low] += 1
        used[high] += 1
    return order


def total_rows(value):
    for by in (4, 2, 1):
        value = value + pltpu.roll(value, by, 0)
    return value


def kernel(
    nx, nz,
    spread_ref, od_ref, th_ref, dr_ref, dp_ref,
    flux_ref, share_ref,
    width_ref, fields, moves, ext, lines, arrived, edge_out, edge_in, row, rows,
    in_sem, edge_ssem, edge_rsem, line_ssem, line_rsem, row_ssem, row_rsem, width_sem, ready,
):
    length, columns, lanes = od_ref.shape
    tiles = columns // 8
    count = nx * nz
    holders = columns // nx
    middle = nx // 4
    order = holder_order(nx, columns)
    groups = line_rsem.shape[0]
    team = count // groups
    inner = length - 2 * REACH
    gx = lax.axis_index("gx")
    gz = lax.axis_index("gz")
    me = gz * nx + gx
    holds = gz < holders
    inner_me = jnp.logical_and(gx >= middle, gx < nx - middle)

    def device(index):
        return {"gx": lax.rem(index, nx), "gz": lax.div(index, nx)}

    def wrap(index, size):
        return jnp.where(index >= size, index - size, index)

    def input_copies(t):
        at = pl.ds(pl.multiple_of(t * 8, 8), 8)
        found = [
            pltpu.make_async_copy(ref.at[:, at, :], fields.at[k, t], in_sem.at[k, t])
            for k, ref in enumerate((od_ref, th_ref, dr_ref))
        ]
        return found + [pltpu.make_async_copy(dp_ref.at[:, at, :], moves.at[t], in_sem.at[3, t])]

    for copy in input_copies(0):
        copy.start()
    width_copy = pltpu.make_async_copy(spread_ref, width_ref, width_sem)
    width_copy.start()

    @pl.loop(1, tiles)
    def _(p):
        for copy in input_copies(p):
            copy.start()

    barrier = pltpu.get_barrier_semaphore()
    for b in range(nz):
        @pl.loop(0 if b else 1, nx)
        def _(a, b=b):
            x = wrap(gx + a, nx)

            @pl.when(jnp.logical_or(inner_me, jnp.logical_or(x < middle, x >= nx - middle)))
            def _():
                pl.semaphore_signal(
                    barrier, inc=1, device_id={"gx": x, "gz": wrap(gz + b, nz)},
                    device_id_type=pl.DeviceIdType.MESH,
                )

    def meet():
        @pl.when(inner_me)
        def _():
            pl.semaphore_wait(barrier, count // 2 - 1)

        @pl.when(jnp.logical_not(inner_me))
        def _():
            pl.semaphore_wait(barrier, count - 1)
            for b in range(nz):
                @pl.loop(0, nx // 2)
                def _(a, b=b):
                    pl.semaphore_signal(
                        ready, inc=1, device_id={"gx": middle + a, "gz": wrap(gz + b, nz)},
                        device_id_type=pl.DeviceIdType.MESH,
                    )

    def meet_rest():
        @pl.when(inner_me)
        def _():
            pl.semaphore_wait(ready, count // 2)

    before = device(lax.rem(me + count - 1, count))
    after = device(lax.rem(me + 1, count))

    def brick_rows(z, t):
        return pl.ds(pl.multiple_of(z * columns + t * 8, 8), 8)

    def line_rows(place, t):
        return pl.ds(t * 8 * length + place, 8, stride=length)

    def tile_masks(t):
        sublane = lax.broadcasted_iota(jnp.int32, (8, lanes), 0)
        width = jnp.zeros((8, lanes), jnp.int32)
        for s in range(8):
            width = jnp.where(sublane == s, width_ref[t * 8 + s], width)
        return [jnp.where(width >= j, 1.0, 0.0).astype(jnp.float32) for j in (2, 3, 4)]

    empty = (jnp.zeros((8, lanes), jnp.float32),) * (2 * REACH)

    def group(t, masks, g, window):
        done = []
        for k in range(8):
            z = g * 8 + k
            terms = spread_terms(fields[0, t, z], fields[1, t, z], fields[2, t, z], masks)
            slots = route(terms, moves[t, z])
            window = [w + s for w, s in zip(window, slots)] + slots[len(window):]
            done.append(window[0])
            window = window[1:]
        return done, tuple(window)

    part = inner // 16 * 8

    def send_lines(t, start, size):
        for tile in range(tiles):
            @pl.when(t == tile)
            def _(tile=tile):
                for column in range(tile * 8, tile * 8 + 8):
                    hx, hz = order[column]

                    @pl.when(hz * nx + hx != me)
                    def _(column=column, hx=hx, hz=hz):
                        pltpu.make_async_remote_copy(
                            src_ref=lines.at[pl.ds(column * length + start, size)],
                            dst_ref=arrived.at[pl.ds(pl.multiple_of(me * length + start, 8), size)],
                            send_sem=line_ssem, recv_sem=line_rsem.at[lax.div(me, team)],
                            device_id={"gx": hx, "gz": hz}, device_id_type=pl.DeviceIdType.MESH,
                        ).start()

    def deposit(t, natural, first):
        masks = tile_masks(t)

        def body(g, window):
            done, window = group(t, masks, g, window)

            @pl.when(jnp.logical_and(g == 0, natural))
            def _():
                for k in range(8):
                    edge_out[1, t, k] = done[k]

            @pl.when(g == 1)
            def _():
                for k in range(8):
                    ext[brick_rows(k, t), :] = done[k]

            @pl.when(g >= 2)
            def _():
                for k in range(8):
                    ext[brick_rows(g * 8 - 8 + k, t), :] = done[k]
                    lines[line_rows(g * 8 - 16 + k, t), :] = done[k]

            @pl.when(jnp.logical_and(first, g == part // 8 + 1))
            def _():
                meet()
                send_lines(0, 0, part)

            return window

        window = lax.fori_loop(0, length // 8, body, empty)
        for k in range(REACH):
            ext[brick_rows(length - REACH + k, t), :] = window[k]

        @pl.when(natural)
        def _():
            for k in range(REACH):
                edge_out[0, t, k] = window[REACH + k]

    def early_edges(t):
        masks = tile_masks(t)

        @pl.loop(0, 2)
        def _(side):
            low = side == 1
            done, window = group(t, masks, jnp.where(low, 0, length // 8 - 1), empty)
            for k in range(REACH):
                edge_out[side, t, k] = jnp.where(low, done[k], window[REACH + k])

    def edge_copies(t):
        return [
            pltpu.make_async_remote_copy(
                src_ref=edge_out.at[k, t], dst_ref=edge_in.at[k, t],
                send_sem=edge_ssem.at[k, t], recv_sem=edge_rsem.at[k, t],
                device_id=target, device_id_type=pl.DeviceIdType.MESH,
            )
            for k, target in enumerate((after, before))
        ]

    width_copy.wait()

    def add_edges(t):
        for copy in edge_copies(t):
            copy.wait_recv()
        for k in range(REACH):
            low = ext[brick_rows(k, t), :] + edge_in[0, t, k]
            ext[brick_rows(k, t), :] = low
            lines[line_rows(inner + k, t), :] = low
            top = ext[brick_rows(length - REACH + k, t), :] + edge_in[1, t, k]
            ext[brick_rows(length - REACH + k, t), :] = top
            lines[line_rows(inner + REACH + k, t), :] = top

    def wait_inputs(t):
        for copy in input_copies(t):
            copy.wait()

    def send_edges(t):
        for copy in edge_copies(t):
            copy.start()

    last = tiles - 1

    @pl.loop(0, tiles)
    def _(p):
        t = p

        @pl.when(p < 2)
        def _():
            wait_inputs(t)

        deposit(t, p < 2, p == 0)

        @pl.when(p == 1)
        def _():
            @pl.loop(2, tiles)
            def _(q):
                wait_inputs(q)
                early_edges(q)

            meet_rest()

            @pl.loop(0, tiles)
            def _(q):
                send_edges(q)

        @pl.when(p == 0)
        def _():
            send_lines(0, part, inner - part)

        @pl.when(jnp.logical_and(p > 0, p < tiles - 1))
        def _():
            send_lines(t, 0, inner)

    @pl.loop(0, tiles)
    def _(p):
        t = p
        add_edges(t)

        @pl.when(p < tiles - 1)
        def _():
            send_lines(t, inner, 2 * REACH)

    send_lines(last, 0, length)

    my_column = 0
    for column, (hx, hz) in enumerate(order):
        my_column = jnp.where(me == hz * nx + hx, column, my_column)

    early = columns - 8
    my_class = jnp.where(my_column >= early, 1, 0)

    def row_copy(target):
        return pltpu.make_async_remote_copy(
            src_ref=row.at[0], dst_ref=rows.at[my_column],
            send_sem=row_ssem, recv_sem=row_rsem.at[my_class],
            device_id=target, device_id_type=pl.DeviceIdType.MESH,
        )

    def wait_bytes(ref, sem):
        pltpu.make_async_copy(ref, ref, sem).wait()

    def block(m, i, sums):
        first, second = list(sums[:4]), list(sums[4:])
        for k in range(length // 8):
            tau = arrived[pl.ds(pl.multiple_of(i * length + 8 * k, 8), 8), :]
            damped = jnp.exp2(m * tau)
            first[k % 4] += damped
            second[k % 4] += tau * damped
        return tuple(first + second)

    @pl.when(holds)
    def _():
        cells = float(count * length)
        zeros = (jnp.zeros((8, lanes), jnp.float32),) * 8

        def next_level(level, factor, sums):
            first = total_rows((sums[0] + sums[1]) + (sums[2] + sums[3]))
            second = total_rows((sums[4] + sums[5]) + (sums[6] + sums[7]))
            return level + (first * (0.4 / cells) - 0.14) / (factor * (second * (1.0 / cells)))

        unit = jnp.full((8, lanes), -LOG2E, jnp.float32)
        own = lax.div(me, team)

        for k in range(length // 8):
            arrived[pl.ds(pl.multiple_of(me * length + 8 * k, 8), 8), :] = lines[
                pl.ds(pl.multiple_of(my_column * length + 8 * k, 8), 8), :
            ]

        def visit(g, sums):
            return lax.fori_loop(0, team, lambda i, sums: block(unit, g * team + i, sums), sums, unroll=min(team, 8))

        wait_bytes(arrived.at[pl.ds(0, (team - 1) * length)], line_rsem.at[own])
        sums = visit(own, zeros)

        def arrive(step, sums):
            g = lax.rem(own + step, groups)
            wait_bytes(arrived.at[pl.ds(0, team * length)], line_rsem.at[g])
            return visit(g, sums)

        sums = lax.fori_loop(1, groups, arrive, sums)
        level = next_level(jnp.zeros((8, lanes), jnp.float32), jnp.ones((8, lanes), jnp.float32), sums)

        def newton(_, level):
            factor = jnp.exp(level)
            m = factor * (-LOG2E)
            sums = lax.fori_loop(0, count, lambda i, sums: block(m, i, sums), zeros, unroll=min(count, 16))
            return next_level(level, factor, sums)

        level = lax.fori_loop(1, ITERS, newton, level)
        row[0] = jnp.exp(level)[0:1]
        rows[my_column] = row[0]

        @pl.loop(0, nx)
        def _(x):
            for b in range(nz):
                @pl.when(jnp.logical_or(x != gx, gz != b))
                def _(b=b):
                    row_copy({"gx": x, "gz": b}).start()

    def wait_rows(kind, size):
        mine = jnp.logical_and(holds, my_class == kind)

        @pl.when(mine)
        def _():
            wait_bytes(rows.at[pl.ds(0, size - 1)], row_rsem.at[kind])

        @pl.when(jnp.logical_not(mine))
        def _():
            wait_bytes(rows.at[pl.ds(0, size)], row_rsem.at[kind])

    def transmit(t):
        m = jnp.concatenate([rows[t * 8 + x] for x in range(8)], axis=0) * (-LOG2E)

        @pl.loop(0, length // 16)
        def _(g):
            for k in range(16):
                at = brick_rows(g * 16 + k, t)
                flux_ref[at, :] = jnp.exp2(m * ext[at, :])

    wait_rows(0, early)

    @pl.loop(0, tiles - 1)
    def _(t):
        transmit(t)

    wait_rows(1, 8)
    transmit(tiles - 1)
    for x in range(share_ref.shape[0]):
        share_ref[x:x + 1, :] = rows[gx * share_ref.shape[0] + x]

    @pl.when(holds)
    def _():
        wait_bytes(lines.at[pl.ds(0, (columns - 1) * length)], line_ssem)
        wait_bytes(arrived.at[pl.ds(0, count - 1)], row_ssem)

    @pl.when(jnp.logical_not(holds))
    def _():
        wait_bytes(lines, line_ssem)

    @pl.loop(0, tiles)
    def _(t):
        for copy in edge_copies(t):
            copy.wait_send()


def deliver(flux_ref, part_ref, flux_out, part_out, sem):
    size = flux_ref.shape[0] // PARTS
    copies = [
        pltpu.make_async_copy(flux_ref.at[pl.ds(i * size, size)], flux_out.at[pl.ds(i * size, size)], sem.at[i])
        for i in range(PARTS)
    ]
    copies.append(pltpu.make_async_copy(part_ref, part_out, sem.at[PARTS]))
    for copy in copies:
        copy.start()
    for copy in copies:
        copy.wait()


def shards(nx, nz, overdensity_ratio, thermal_state, residual_drift, peculiar_displacement, doppler_spread):
    _, length, columns, lanes = overdensity_ratio.shape
    tiles = columns // 8
    count = nx * nz
    assert columns % 16 == 0 and nx % 4 == 0 and columns % nx == 0 and columns // nx <= nz
    assert 8 % (columns // nx) == 0
    assert length % 16 == 0 and length > 2 * REACH and count % GROUPS == 0 and count > GROUPS
    f32 = jnp.float32
    scratch = [
        pltpu.SMEM((columns,), jnp.int32),
        pltpu.VMEM((3, tiles, length, 8, lanes), f32),
        pltpu.VMEM((tiles, length, 8, lanes), jnp.int32),
        pltpu.VMEM((length * columns, lanes), f32),
        pltpu.VMEM((columns * length, lanes), f32),
        pltpu.VMEM((count * length, lanes), f32),
        pltpu.VMEM((2, tiles, REACH, 8, lanes), f32),
        pltpu.VMEM((2, tiles, REACH, 8, lanes), f32),
        pltpu.VMEM((1, 1, lanes), f32),
        pltpu.VMEM((columns, 1, lanes), f32),
        pltpu.SemaphoreType.DMA((4, tiles)),
        pltpu.SemaphoreType.DMA((2, tiles)),
        pltpu.SemaphoreType.DMA((2, tiles)),
        pltpu.SemaphoreType.DMA(()),
        pltpu.SemaphoreType.DMA((GROUPS,)),
        pltpu.SemaphoreType.DMA(()),
        pltpu.SemaphoreType.DMA((2,)),
        pltpu.SemaphoreType.DMA(()),
        pltpu.SemaphoreType.REGULAR,
    ]
    used = 4 * lanes * (columns * length * 6 + 2 * REACH * columns * 4 + count * length)
    bricks = [
        pltpu.with_memory_space_constraint(value[0], pltpu.HBM)
        for value in (overdensity_ratio, thermal_state, residual_drift, peculiar_displacement)
    ]
    flux, part = pl.pallas_call(
        functools.partial(kernel, nx, nz),
        out_shape=(
            jax.ShapeDtypeStruct((length * columns, lanes), f32),
            jax.ShapeDtypeStruct((columns // nx, lanes), f32),
        ),
        in_specs=[pl.BlockSpec(memory_space=pltpu.HBM)] * 5,
        out_specs=(pl.BlockSpec(memory_space=pltpu.VMEM), pl.BlockSpec(memory_space=pltpu.VMEM)),
        scratch_shapes=scratch,
        compiler_params=pltpu.CompilerParams(
            collective_id=0, has_side_effects=True, vmem_limit_bytes=used + 4 * lanes * columns * length + (4 << 20)
        ),
        name="forest",
    )(pltpu.with_memory_space_constraint(doppler_spread, pltpu.HBM), *bricks)
    flux, part = pl.pallas_call(
        deliver,
        out_shape=(
            jax.ShapeDtypeStruct((length * columns, lanes), f32),
            jax.ShapeDtypeStruct((columns // nx, lanes), f32),
        ),
        in_specs=[pl.BlockSpec(memory_space=pl.ANY)] * 2,
        out_specs=(pl.BlockSpec(memory_space=pltpu.HBM), pl.BlockSpec(memory_space=pltpu.HBM)),
        scratch_shapes=[pltpu.SemaphoreType.DMA((PARTS + 1,))],
        compiler_params=pltpu.CompilerParams(vmem_limit_bytes=1 << 20),
        name="deliver",
    )(flux, part)
    return flux.reshape(1, length, columns, lanes), part


def solution(mesh):
    placed = (
        P("gz", "gx", None, None),
        P("gz", "gx", None, None),
        P("gz", "gx", None, None),
        P("gz", "gx", None, None),
        P(),
    )
    return jax.shard_map(
        functools.partial(shards, mesh.shape["gx"], mesh.shape["gz"]),
        mesh=mesh,
        in_specs=placed,
        out_specs=(P("gz", "gx", None, None), P("gx", None)),
        check_vma=False,
    )
```
